128 devices in a mesh: rows: 16 (over z, y), cols: 4 (over x_lo, core), layers: 2 (over x_hi).
Axes of the slice: x: 4 (x_hi: 2, x_lo: 2; x = x_hi * 2 + x_lo), y: 4, z: 4, core: 2. Of those that a mesh axis runs over, the one named last changes fastest.
Arguments:
- term_now: bfloat16 [384, 128, 2048], P('rows', 'layers', 'cols'), may hold values from -6 to 6
- term_prev: bfloat16 [384, 128, 2048], P('rows', 'layers', 'cols'), may hold values from -6 to 6
- cotangent: bfloat16 [384, 128, 2048], P('rows', None, 'cols'), may hold values from -6 to 6
- ham_blocks: bfloat16 [384, 25, 128, 128], P('rows', None, 'layers'), as said below
- block_mask: int32 [384, 25], P('rows'), may hold values from 0 to 1, as said below
- ham_slope: bfloat16 [384, 25, 128, 128], P('rows', None, 'layers'), may hold values from -0.0012207031 to 0.0012207031
- atom_owner: int32 [384, 128], P('rows'), may hold values from 0 to 63, never falling along the last dimension, each value on 1 to 4 neighbouring positions
Outputs:
- term_next: bfloat16 [384, 128, 2048], P('rows', 'layers', 'cols')
- grad_term: bfloat16 [384, 128, 2048], P('rows', 'layers', 'cols')
- forces: float32 [384, 64], P('rows')
The draws below stay inside these ranges and needn't reach their ends.
Inputs may be any that keep to these rules, and one draw needn't show every extreme that they name: ham_blocks[i, d] is the transpose of ham_blocks[(i + d - 12) mod 384, 24 - d]: H is symmetric. block_mask[i, d] equals block_mask[(i + d - 12) mod 384, 24 - d], and block_mask[i, 12] is 1. Each row of atom_owner never falls; each atom owns 1 to 4 consecutive row orbitals.
All inputs are finite; a program needn't handle non-finite values.
Results may differ from the reference program's by a relative error of at most 0.005.
Values may be sent and summed in bfloat16 or wider, within the bound.
A program may use at most 128 MiB of HBM per device.

```python
import math
import jax
import jax.numpy as jnp
import numpy as np
from jax import lax

B = 128
R = 12
SLOTS = 25
NB = 384
NCOL = 2048
APB = 64
N_LAYERS = 2


def draw_ham_blocks(key, part):
    full_shape = (NB, SLOTS, B, B)
    noise = jax.random.normal(key, full_shape, jnp.float32)
    row_ids = jnp.arange(NB)[:, None]
    slot_ids = jnp.arange(SLOTS)[None, :]
    partner = (row_ids + slot_ids - R) % NB
    mirror = noise[partner, SLOTS - 1 - slot_ids]
    symmetric = (noise + jnp.swapaxes(mirror, 2, 3)) * (0.5 / math.sqrt(2.0 * SLOTS * B))
    return symmetric.astype(jnp.bfloat16)


def draw_block_mask(key, part):
    raw_draw = jax.random.randint(key, (NB, SLOTS), 0, 100)
    slot_ids = jnp.arange(SLOTS)[None, :]
    row_ids = jnp.arange(NB)[:, None]
    distance = jnp.abs(slot_ids - R)
    kept = (raw_draw < 100 - 50 * distance // R).astype(jnp.int32)
    partner = (row_ids + slot_ids - R) % NB
    mirrored = kept[partner, SLOTS - 1 - slot_ids]
    return jnp.where(slot_ids >= R, kept, mirrored).astype(jnp.int32)


def levels(stream_key, shape, cuts, low, largest):
    def one(axis_at, blocks):
        draws = jax.random.uniform(jax.random.fold_in(jax.random.fold_in(stream_key, 6), axis_at), (blocks,), jnp.float32, low / len(cuts), largest / len(cuts))
        return jnp.repeat(jnp.exp(draws), shape[axis_at] // blocks).reshape((-1,) + (1,) * (len(shape) - axis_at - 1))

    level = one(*cuts[0])
    for cut in cuts[1:]:
        level = level * one(*cut)
    return level


def split_up(count, total, reach, lean):
    weights = [(1 << 20) // math.isqrt(standing ** lean) + 1 for standing in range(2, count + 1)]
    rest, holding = total - reach - (count - 1), [1] * (count - 1)
    while rest > 0:
        movable = [i for i in range(count - 1) if holding[i] < reach]
        pool, remaining = sum([weights[i] for i in movable]), rest
        for i in movable:
            more = min(reach - holding[i], max(1, remaining * weights[i] // pool), rest)
            holding[i] = holding[i] + more
            rest = rest - more
    return np.array([reach] + holding)


def uneven(rng, count, total, limit, slope):
    if count == 2:
        one = jax.random.randint(rng, (), max(1, total - limit), min(limit, total - 1) + 1)
        return jnp.stack([one, total - one])
    lengths = jnp.asarray(split_up(count, total, limit, slope), jnp.int32)
    couples = (count - 1) // 2
    source_of, sink = lengths[1:1 + 2 * couples:2], lengths[2:2 + 2 * couples:2]
    slack = jnp.minimum(source_of - 1, limit - sink)
    moved = jax.random.randint(jax.random.fold_in(rng, 1), (couples,), 0, 1 << 20) % (slack + 1)
    lengths = lengths.at[1:1 + 2 * couples:2].set(source_of - moved).at[2:2 + 2 * couples:2].set(sink + moved)
    return lengths[jax.random.permutation(jax.random.fold_in(rng, 2), count)]


def centred(stream_key, dims, width, limit, cuts=(), held_as=jnp.bfloat16):
    factor_of = levels(stream_key, dims, cuts, -0.22, 0.18) if cuts else 1.0
    result = jax.random.normal(stream_key, dims, jnp.float32) * width * factor_of
    return jnp.minimum(jnp.maximum(result, -limit), limit).astype(held_as)


def setup_inputs(seed: int = 0) -> dict:
    splits = jax.random.split(jax.random.key(seed), 8)
    return {
        "term_now": centred(splits[0], (NB, B, NCOL), 1.0, 6.0, ((0, 16), (1, 2), (2, 4))),
        "term_prev": centred(splits[1], (NB, B, NCOL), 1.0, 6.0, ((0, 16), (1, 2), (2, 4))),
        "cotangent": centred(splits[2], (NB, B, NCOL), 1.0, 6.0, ((0, 16), (2, 4))),
        "ham_blocks": draw_ham_blocks(jax.random.fold_in(splits[7], 71), 0),
        "block_mask": draw_block_mask(jax.random.fold_in(splits[7], 71), 0),
        "ham_slope": centred(splits[5], (NB, SLOTS, B, B), (4 * SLOTS * B * NCOL) ** -0.5, 0.0012207031, ((0, 16), (2, 2))),
        "atom_owner": jax.vmap(lambda own: jnp.searchsorted(jnp.cumsum(uneven(own, APB, B, 4, 0)), jnp.arange(B), side="right"))(jax.random.split(splits[6], NB)).reshape((NB, B)).astype(jnp.int32),
    }


def reference(term_now, term_prev, cotangent, ham_blocks, block_mask, ham_slope, atom_owner):
    half_rows = B // N_LAYERS
    state = term_now.astype(jnp.float32)
    cot_float = cotangent.astype(jnp.float32)
    mask_float = block_mask.astype(jnp.float32)

    def advance(offset, sums):
        forward, backward, row_force = sums
        kept = lax.dynamic_index_in_dim(mask_float, offset, 1, keepdims=False)
        masked = lax.dynamic_index_in_dim(ham_blocks, offset, 1, keepdims=False).astype(jnp.float32)
        masked = masked * kept[:, None, None]
        nearby = jnp.roll(state, R - offset, axis=0)
        split_blocks = masked.reshape(NB, N_LAYERS, half_rows, B)
        split_state = nearby.reshape(NB, N_LAYERS, half_rows, NCOL)
        forward = forward + jnp.einsum("ihnm,ihnc->himc", split_blocks, split_state)
        split_cols = masked.reshape(NB, B, N_LAYERS, half_rows)
        split_cot = cot_float.reshape(NB, N_LAYERS, half_rows, NCOL)
        sources = jnp.einsum("inhm,ihmc->hinc", split_cols, split_cot)
        backward = backward + jnp.roll(sources, offset - R, axis=1)
        pair_grads = 2.0 * kept[:, None, None] * jnp.einsum("inc,imc->inm", nearby, cot_float)
        slope_block = lax.dynamic_index_in_dim(ham_slope, offset, 1, keepdims=False).astype(jnp.float32)
        row_force = row_force + jnp.sum(pair_grads * slope_block, axis=1)
        return forward, backward, row_force

    zeros_terms = jnp.zeros((N_LAYERS, NB, B, NCOL), jnp.float32)
    initial = (zeros_terms, zeros_terms, jnp.zeros((NB, B), jnp.float32))
    forward, backward, row_force = lax.fori_loop(0, SLOTS, advance, initial)
    forward_sum = jnp.sum(forward, axis=0)
    backward_sum = jnp.sum(backward, axis=0)
    term_next = (2.0 * forward_sum - term_prev.astype(jnp.float32)).astype(jnp.bfloat16)
    grad_term = (2.0 * backward_sum).astype(jnp.bfloat16)
    atom_ids = jnp.arange(APB, dtype=jnp.int32)
    owners = (atom_owner[:, :, None] == atom_ids[None, None, :]).astype(jnp.float32)
    forces = jnp.einsum("im,ima->ia", row_force, owners)
    return term_next, grad_term, forces
```

```python
import jax
import jax.numpy as jnp
from jax import lax
from jax.experimental import pallas as pl
from jax.experimental.pallas import tpu as pltpu
from jax.sharding import PartitionSpec as P

BF = jnp.bfloat16
F32 = jnp.float32
MESH = pl.DeviceIdType.MESH

ROWS = 24
HALF = 64
ORB = 128
COLS = 512
SLOTS = 25
REACH = 12
STEPS = 6


def remote(src, dst, send_sem, recv_sem, device):
    return pltpu.make_async_remote_copy(
        src_ref=src, dst_ref=dst, send_sem=send_sem, recv_sem=recv_sem,
        device_id=device, device_id_type=MESH,
    )


def kernel(
    mask, owner, tn, tp, cot_h, ham_h, slope_h,
    tno, gro, fo,
    ext, tt, cot, ham, slope, own, xs, xr, bown, bs, br, prev, to, go, rf, fbuf,
    lsem, hsem, osem, hs, hr, xss, xrs, bss, bsr, fs, fr,
):
    row = lax.axis_index("rows")
    col = lax.axis_index("cols")
    lay = lax.axis_index("layers")
    up = {"rows": lax.rem(row + 1, 16)}
    down = {"rows": lax.rem(row + 15, 16)}
    partner = {"layers": 1 - lay}
    me = col * 2 + lay

    def ring(index):
        return {"cols": index // 2, "layers": index % 2}

    barrier = pltpu.get_barrier_semaphore()
    pl.semaphore_signal(barrier, 1, device_id=up, device_id_type=MESH)
    pl.semaphore_signal(barrier, 1, device_id=down, device_id_type=MESH)
    for o in range(1, 8):
        pl.semaphore_signal(
            barrier, 1, device_id=ring(lax.rem(me + o, 8)), device_id_type=MESH
        )

    def load_term():
        return pltpu.make_async_copy(tn, ext.at[pl.ds(REACH, ROWS)], lsem.at[0])

    def load_cot():
        return pltpu.make_async_copy(cot_h, cot, lsem.at[1])

    def load_prev():
        return pltpu.make_async_copy(tp, prev, lsem.at[2])

    def load_blocks(k):
        copies = []
        for side, first in ((0, 10 - 2 * k), (1, 12 + 2 * k)):
            at = pl.ds(first, 2)
            copies.append(pltpu.make_async_copy(ham_h.at[at], ham.at[at], hsem.at[0, side, k]))
            copies.append(
                pltpu.make_async_copy(slope_h.at[at], slope.at[at], hsem.at[1, side, k])
            )
        return copies

    load_term().start()
    for c in load_blocks(0):
        c.start()
    load_cot().start()
    for k in range(1, STEPS):
        for c in load_blocks(k):
            c.start()
    load_prev().start()

    def to_up(k):
        return remote(
            tn.at[pl.ds(22 - 2 * k, 2)], ext.at[pl.ds(10 - 2 * k, 2)],
            hs.at[0, k], hr.at[0, k], up,
        )

    def to_down(k):
        return remote(
            tn.at[pl.ds(2 * k, 2)], ext.at[pl.ds(36 + 2 * k, 2)],
            hs.at[1, k], hr.at[1, k], down,
        )

    pl.semaphore_wait(barrier, 9)
    for k in range(STEPS):
        to_up(k).start()
        to_down(k).start()

    def turn(pair):
        tt[pair] = ext[pl.ds(2 * pair, 2)].reshape(ORB, COLS).T

    load_term().wait()

    def turn_local(p, carry):
        turn(p + 6)
        return carry

    lax.fori_loop(0, 12, turn_local, 0)

    def mask_rows(k, carry):
        for c in load_blocks(k):
            c.wait()
        for first in (10 - 2 * k, 12 + 2 * k):
            for r in range(2):
                i = first + r
                for d in range(SLOTS):
                    kept = jnp.full((HALF, ORB), mask[i, d].astype(F32), F32).astype(BF)
                    ham[i, d] = ham[i, d] * kept
                    slope[i, d] = slope[i, d] * kept
        return carry

    def send_partial(k, side):
        at = pl.ds(10 - 2 * k if side == 0 else 12 + 2 * k, 2)
        return remote(
            xs.at[at], xr.at[at], xss.at[side, k], xrs.at[side, k], partner
        )

    def forward(k, carry):
        to_up(k).wait_recv()
        to_down(k).wait_recv()
        turn(5 - k)
        turn(18 + k)
        for side in range(2):
            pair = 5 - k if side == 0 else 6 + k
            lhs = jnp.concatenate([tt[pair + g] for g in range(13)], axis=1)
            edge = jnp.zeros((HALF, 2 * ORB), BF)
            weights = []
            for r in range(2):
                i = 2 * pair + r
                w = jnp.concatenate(
                    [
                        ham[i].reshape(SLOTS * HALF, ORB),
                        slope[i].reshape(SLOTS * HALF, ORB),
                    ],
                    axis=1,
                )
                weights.append(jnp.concatenate([edge, w] if r else [w, edge], axis=0))
            out = jnp.dot(
                lhs, jnp.concatenate(weights, axis=1), preferred_element_type=F32
            )
            for r in range(2):
                i = 2 * pair + r
                f = out[:, 2 * r * ORB : (2 * r + 1) * ORB].T
                low, high = f[:HALF], f[HALF:]
                own[i] = jnp.where(lay == 0, low, high)
                xs[i] = jnp.where(lay == 0, high, low).astype(BF)
                g = out[:, (2 * r + 1) * ORB : (2 * r + 2) * ORB]
                turned = cot[i].T.astype(F32)
                rf[i] = 2.0 * jnp.sum(turned * g, axis=0, keepdims=True)
            send_partial(k, side).start()
        return carry

    def push_group(g):
        i0, i1 = max(0, 4 * g - 24), min(ROWS - 1, 4 * g + 3)
        parts = []
        for i in range(i0, i1 + 1):
            d0 = 4 * g - i
            lo, hi = max(0, -d0), min(4, SLOTS - d0)
            p = []
            if lo:
                p.append(jnp.zeros((HALF * lo, ORB), BF))
            p.append(ham[i, d0 + lo : d0 + hi].reshape((hi - lo) * HALF, ORB))
            if hi < 4:
                p.append(jnp.zeros((HALF * (4 - hi), ORB), BF))
            parts.append(jnp.concatenate(p, axis=0) if len(p) > 1 else p[0])
        out = jnp.dot(
            jnp.concatenate(parts, axis=1),
            cot[i0 : i1 + 1].reshape((i1 - i0 + 1) * ORB, COLS),
            preferred_element_type=F32,
        )
        return out.reshape(4, HALF, COLS)

    def send_pushed(side, g):
        at = pl.ds(4 * g, 4)
        return remote(
            bs.at[side, at], br.at[1 - side, at], bss.at[side, g], bsr.at[side, g],
            down if side == 0 else up,
        )

    mask_rows(0, 0)
    load_cot().wait()
    forward(0, 0)
    lax.fori_loop(1, STEPS, mask_rows, 0)
    for g in range(3):
        bs[0, 4 * g : 4 * g + 4] = push_group(g).astype(BF)
        bs[1, 4 * g : 4 * g + 4] = push_group(9 + g).astype(BF)
        send_pushed(0, g).start()
        send_pushed(1, g).start()
    lax.fori_loop(1, STEPS, forward, 0)

    atoms = lax.broadcasted_iota(jnp.int32, (HALF, ORB), 0)
    lanes = lax.broadcasted_iota(jnp.int32, (HALF, ORB), 1)

    def gather_atoms(i, total):
        mine = jnp.where(owner[pl.ds(i, 1)] == atoms, rf[i], 0.0)
        summed = jnp.sum(mine, axis=1, keepdims=True)
        return total + jnp.where(lanes == i, summed, 0.0)

    total = lax.fori_loop(0, ROWS, gather_atoms, jnp.zeros((HALF, ORB), F32))
    total = jnp.concatenate([total, jnp.zeros((HALF, ORB), F32)], axis=0).T
    fbuf[me] = total[:ROWS]

    def send_force(o):
        return remote(
            fbuf.at[me], fbuf.at[me], fs.at[o - 1], fr.at[o - 1],
            ring(lax.rem(me + o, 8)),
        )

    def take_force(o):
        slot = lax.rem(me + 8 - o, 8)
        return remote(
            fbuf.at[slot], fbuf.at[slot], fs.at[o - 1], fr.at[o - 1],
            ring(lax.rem(me + o, 8)),
        )

    for o in range(1, 8):
        send_force(o).start()

    for g in range(3, 9):
        bown[4 * (g - 3) : 4 * (g - 2)] = push_group(g)

    for o in range(1, 8):
        take_force(o).wait_recv()
    summed = fbuf[0]
    for s in range(1, 8):
        summed = summed + fbuf[s]
    fo[...] = summed[:, :HALF]

    load_prev().wait()

    def out_term(k, side):
        at = pl.ds(10 - 2 * k if side == 0 else 12 + 2 * k, 2)
        return pltpu.make_async_copy(to.at[at], tno.at[at], osem.at[side, k])

    def out_grad(side, g):
        at = pl.ds(12 * side + 4 * g, 4)
        return pltpu.make_async_copy(go.at[at], gro.at[at], osem.at[side, STEPS + g])

    def finish_term(k, carry):
        for side in range(2):
            at = pl.ds(10 - 2 * k if side == 0 else 12 + 2 * k, 2)
            send_partial(k, side).wait_recv()
            both = own[at] + xr[at].astype(F32)
            to[at] = (2.0 * both - prev[at].astype(F32)).astype(BF)
            out_term(k, side).start()
        return carry

    def finish_grad(g):
        for side in range(2):
            at = pl.ds(12 * side + 4 * g, 4)
            send_pushed(1 - side, g).wait_recv()
            both = bown[at] + br[side, pl.ds(4 * g, 4)].astype(F32)
            go[at] = (2.0 * both).astype(BF)
            out_grad(side, g).start()

    lax.fori_loop(0, 3, finish_term, 0)
    finish_grad(0)
    finish_term(3, 0)
    finish_grad(1)
    finish_term(4, 0)
    finish_grad(2)
    finish_term(5, 0)

    for k in range(STEPS):
        to_up(k).wait_send()
        to_down(k).wait_send()
        for side in range(2):
            send_partial(k, side).wait_send()
            out_term(k, side).wait()
    for g in range(3):
        for side in range(2):
            send_pushed(side, g).wait_send()
            out_grad(side, g).wait()
    for o in range(1, 8):
        send_force(o).wait_send()


def local(term_now, term_prev, cotangent, ham_blocks, block_mask, ham_slope, atom_owner):
    anyspace = pl.BlockSpec(memory_space=pl.ANY)
    dma = pltpu.SemaphoreType.DMA
    block = (ROWS, HALF, COLS)
    return pl.pallas_call(
        kernel,
        out_shape=(
            jax.ShapeDtypeStruct(block, BF),
            jax.ShapeDtypeStruct(block, BF),
            jax.ShapeDtypeStruct((ROWS, HALF), F32),
        ),
        in_specs=[
            pl.BlockSpec(memory_space=pltpu.SMEM),
            pl.BlockSpec(memory_space=pltpu.VMEM),
            anyspace, anyspace, anyspace, anyspace, anyspace,
        ],
        out_specs=(anyspace, anyspace, pl.BlockSpec(memory_space=pltpu.VMEM)),
        scratch_shapes=[
            pltpu.VMEM((ROWS + 2 * REACH, HALF, COLS), BF),
            pltpu.VMEM((24, COLS, ORB), BF),
            pltpu.VMEM((ROWS, ORB, COLS), BF),
            pltpu.VMEM((ROWS, SLOTS, HALF, ORB), BF),
            pltpu.VMEM((ROWS, SLOTS, HALF, ORB), BF),
            pltpu.VMEM(block, F32),
            pltpu.VMEM(block, BF),
            pltpu.VMEM(block, BF),
            pltpu.VMEM(block, F32),
            pltpu.VMEM((2, REACH, HALF, COLS), BF),
            pltpu.VMEM((2, REACH, HALF, COLS), BF),
            pltpu.VMEM(block, BF),
            pltpu.VMEM(block, BF),
            pltpu.VMEM(block, BF),
            pltpu.VMEM((ROWS, 1, ORB), F32),
            pltpu.VMEM((8, ROWS, ORB), F32),
            dma((3,)), dma((2, 2, STEPS)), dma((2, STEPS + 3)),
            dma((2, STEPS)), dma((2, STEPS)),
            dma((2, STEPS)), dma((2, STEPS)),
            dma((2, 3)), dma((2, 3)),
            dma((7,)), dma((7,)),
        ],
        compiler_params=pltpu.CompilerParams(
            collective_id=0, has_side_effects=True, vmem_limit_bytes=62_000_000
        ),
        name="chebyshev",
    )(block_mask, atom_owner, term_now, term_prev, cotangent, ham_blocks, ham_slope)


def solution(mesh):
    return jax.shard_map(
        local,
        mesh=mesh,
        in_specs=(
            P("rows", "layers", "cols"),
            P("rows", "layers", "cols"),
            P("rows", None, "cols"),
            P("rows", None, "layers", None),
            P("rows", None),
            P("rows", None, "layers", None),
            P("rows", None),
        ),
        out_specs=(P("rows", "layers", "cols"), P("rows", "layers", "cols"), P("rows", None)),
        check_vma=False,
    )
```

```python
import jax
import jax.numpy as jnp
from jax import lax
from jax.experimental import pallas as pl
from jax.experimental.pallas import tpu as pltpu
from jax.sharding import PartitionSpec as P

BF = jnp.bfloat16
F32 = jnp.float32
MESH = pl.DeviceIdType.MESH

ROWS = 24
HALF = 64
ORB = 128
COLS = 512
SLOTS = 25
REACH = 12
STEPS = 6


def remote(src, dst, send_sem, recv_sem, device):
    return pltpu.make_async_remote_copy(
        src_ref=src, dst_ref=dst, send_sem=send_sem, recv_sem=recv_sem,
        device_id=device, device_id_type=MESH,
    )


def kernel(
    mask_h, owner_h, tn, tp, cot_h, ham_h, slope_h,
    tno, gro, fo,
    mask, owner, ext, tt, cot, ham, slope, own, xs, xr, bown, bs, br, prev, rf, fbuf,
    lsem, csem, hsem, hs, hr, xss, xrs, bss, bsr, fs, fr,
):
    row = lax.axis_index("rows")
    col = lax.axis_index("cols")
    lay = lax.axis_index("layers")
    up = {"rows": lax.rem(row + 1, 16)}
    down = {"rows": lax.rem(row + 15, 16)}
    partner = {"layers": 1 - lay}
    me = col * 2 + lay

    def ring(index):
        return {"cols": index // 2, "layers": index % 2}

    def load_term():
        return pltpu.make_async_copy(tn, ext.at[pl.ds(REACH, ROWS)], lsem.at[0])

    def load_mask():
        return pltpu.make_async_copy(mask_h, mask, lsem.at[2])

    def load_owner():
        return pltpu.make_async_copy(owner_h, owner, lsem.at[3])

    load_term().start()
    barrier = pltpu.get_barrier_semaphore()
    pl.semaphore_signal(barrier, 1, device_id=up, device_id_type=MESH)
    pl.semaphore_signal(barrier, 1, device_id=down, device_id_type=MESH)
    for o in range(1, 8):
        pl.semaphore_signal(
            barrier, 1, device_id=ring(lax.rem(me + o, 8)), device_id_type=MESH
        )

    def load_cot(part):
        at = (pl.ds(10, 4), pl.ds(0, 10), pl.ds(14, 10))[part]
        return pltpu.make_async_copy(cot_h.at[at], cot.at[at], csem.at[part])

    def load_prev():
        return pltpu.make_async_copy(tp, prev, lsem.at[1])

    def load_blocks(k):
        copies = []
        for side, first in ((0, 10 - 2 * k), (1, 12 + 2 * k)):
            at = pl.ds(first, 2)
            copies.append(pltpu.make_async_copy(ham_h.at[at], ham.at[at], hsem.at[0, side, k]))
            copies.append(
                pltpu.make_async_copy(slope_h.at[at], slope.at[at], hsem.at[1, side, k])
            )
        return copies

    load_mask().start()
    for c in load_blocks(0):
        c.start()
    load_cot(0).start()

    def rows_of(s, lone):
        return (1 - s, 1) if lone else (2 - 2 * s, 2)

    def to_up(s, lone):
        back, n = rows_of(s, lone)
        return remote(
            tn.at[pl.ds(22 + back, n)] if lone else ext.at[pl.ds(34 + back, n)], ext.at[pl.ds(10 + back, n)],
            hs.at[0, s], hr.at[0, s], up,
        )

    def to_down(s, lone):
        n = 1 if lone else 2
        on = s if lone else 2 * s - 2
        return remote(
            tn.at[pl.ds(on, n)] if lone else ext.at[pl.ds(12 + on, n)], ext.at[pl.ds(36 + on, n)],
            hs.at[1, s], hr.at[1, s], down,
        )

    with jax.named_scope("rg_barrier"):
        pl.semaphore_wait(barrier, 9)
    for s in range(2):
        to_up(s, True).start()
        to_down(s, True).start()
    with jax.named_scope("rg_term"):
        load_term().wait()
    for s in range(2, STEPS + 1):
        to_up(s, False).start()
        to_down(s, False).start()
    load_cot(1).start()
    load_cot(2).start()
    for k in range(1, STEPS):
        for c in load_blocks(k):
            c.start()
    load_prev().start()
    load_owner().start()

    def turn(pair):
        tt[pair] = ext[pl.ds(2 * pair, 2)].reshape(ORB, COLS).T

    def turn_local(p, carry):
        turn(p + 6)
        return carry

    lax.fori_loop(0, 12, turn_local, 0)

    def mask_rows(k, carry):
        for c in load_blocks(k):
            c.wait()
        for first in (10 - 2 * k, 12 + 2 * k):
            for r in range(2):
                i = first + r
                for d in range(SLOTS):
                    kept = jnp.full((HALF, ORB), mask[i, d].astype(F32), F32).astype(BF)
                    ham[i, d] = ham[i, d] * kept
                    slope[i, d] = slope[i, d] * kept
        return carry

    def send_partial(s, side, lone):
        n = 1 if lone else 2
        first = (11 - s if lone else 12 - 2 * s) if side == 0 else (12 + s if lone else 10 + 2 * s)
        at = pl.ds(first, n)
        return remote(
            xs.at[at], xr.at[at], xss.at[side, s], xrs.at[side, s], partner
        )

    edge = jnp.zeros((HALF, 2 * ORB), BF)

    def stacked(i, before, after):
        w = jnp.concatenate(
            [ham[i].reshape(SLOTS * HALF, ORB), slope[i].reshape(SLOTS * HALF, ORB)],
            axis=1,
        )
        parts = [w]
        if before:
            parts = [jnp.zeros((HALF * before, 2 * ORB), BF)] + parts
        if after:
            parts = parts + [jnp.zeros((HALF * after, 2 * ORB), BF)]
        return jnp.concatenate(parts, axis=0)

    def product(pair, pairs, rows):
        lhs = jnp.concatenate([tt[pair + g] for g in range(pairs)], axis=1)
        weights = [stacked(i, r, 2 * pairs - SLOTS - r) for i, r in rows]
        out = jnp.dot(lhs, jnp.concatenate(weights, axis=1), preferred_element_type=F32)
        for n, (i, _) in enumerate(rows):
            f = out[:, 2 * n * ORB : (2 * n + 1) * ORB].T
            low, high = f[:HALF], f[HALF:]
            own[i] = jnp.where(lay == 0, low, high)
            xs[i] = jnp.where(lay == 0, high, low).astype(BF)
            g = out[:, (2 * n + 1) * ORB : (2 * n + 2) * ORB]
            turned = cot[i].T.astype(F32)
            rf[i] = 2.0 * jnp.sum(turned * g, axis=0, keepdims=True)

    def forward(s, carry):
        to_up(s, False).wait_recv()
        to_down(s, False).wait_recv()
        turn(6 - s)
        turn(17 + s)
        for side in range(2):
            pair = 6 - s if side == 0 else 5 + s
            product(pair, 13, ((2 * pair, 0), (2 * pair + 1, 1)))

            @pl.when(s < STEPS)
            def _():
                send_partial(s, side, False).start()

        return carry

    def push_group(g):
        i0, i1 = max(0, 4 * g - 24), min(ROWS - 1, 4 * g + 3)
        parts = []
        for i in range(i0, i1 + 1):
            d0 = 4 * g - i
            lo, hi = max(0, -d0), min(4, SLOTS - d0)
            p = []
            if lo:
                p.append(jnp.zeros((HALF * lo, ORB), BF))
            p.append(ham[i, d0 + lo : d0 + hi].reshape((hi - lo) * HALF, ORB))
            if hi < 4:
                p.append(jnp.zeros((HALF * (4 - hi), ORB), BF))
            parts.append(jnp.concatenate(p, axis=0) if len(p) > 1 else p[0])
        out = jnp.dot(
            jnp.concatenate(parts, axis=1),
            cot[i0 : i1 + 1].reshape((i1 - i0 + 1) * ORB, COLS),
            preferred_element_type=F32,
        )
        return out.reshape(4, HALF, COLS)

    def send_pushed(side, g):
        at = pl.ds(4 * g, 4)
        return remote(
            bs.at[side, at], br.at[1 - side, at], bss.at[side, g], bsr.at[side, g],
            down if side == 0 else up,
        )

    with jax.named_scope("rg_mask0"):
        load_mask().wait()
        mask_rows(0, 0)
    load_cot(0).wait()
    nothing = jnp.zeros((HALF, COLS), BF)
    with jax.named_scope("rg_halo0"):
        to_up(0, True).wait_recv()
        to_down(0, True).wait_recv()
    with jax.named_scope("rg_fwd0"):
        tt[5] = jnp.concatenate([nothing, ext[11]], axis=0).T
        tt[18] = jnp.concatenate([ext[36], nothing], axis=0).T
        product(5, 14, ((11, 1), (12, 2)))
        for side in range(2):
            send_partial(0, side, True).start()
    with jax.named_scope("rg_halo1"):
        to_up(1, True).wait_recv()
        to_down(1, True).wait_recv()
    with jax.named_scope("rg_fwd1"):
        turn(5)
        turn(18)
        product(5, 14, ((10, 0), (13, 3)))
        for side in range(2):
            send_partial(1, side, True).start()
    with jax.named_scope("rg_mask1"):
        load_cot(1).wait()
        load_cot(2).wait()
        lax.fori_loop(1, STEPS, mask_rows, 0)
    with jax.named_scope("rg_fwd2"):
        forward(2, 0)
    with jax.named_scope("rg_edges"):
        for g in range(3):
            bs[0, 4 * g : 4 * g + 4] = push_group(g).astype(BF)
            bs[1, 4 * g : 4 * g + 4] = push_group(9 + g).astype(BF)
            send_pushed(0, g).start()
            send_pushed(1, g).start()
    with jax.named_scope("rg_fwd"):
        lax.fori_loop(3, STEPS + 1, forward, 0)
    load_owner().wait()

    atoms = lax.broadcasted_iota(jnp.int32, (HALF, ORB), 0)
    lanes = lax.broadcasted_iota(jnp.int32, (HALF, ORB), 1)

    def gather_atoms(i, total):
        mine = jnp.where(owner[pl.ds(i, 1)] == atoms, rf[i], 0.0)
        summed = jnp.sum(mine, axis=1, keepdims=True)
        return total + jnp.where(lanes == i, summed, 0.0)

    total = lax.fori_loop(0, ROWS, gather_atoms, jnp.zeros((HALF, ORB), F32))
    total = jnp.concatenate([total, jnp.zeros((HALF, ORB), F32)], axis=0).T
    fbuf[me] = total[:ROWS]

    def send_force(o):
        return remote(
            fbuf.at[me], fbuf.at[me], fs.at[o - 1], fr.at[o - 1],
            ring(lax.rem(me + o, 8)),
        )

    def take_force(o):
        slot = lax.rem(me + 8 - o, 8)
        return remote(
            fbuf.at[slot], fbuf.at[slot], fs.at[o - 1], fr.at[o - 1],
            ring(lax.rem(me + o, 8)),
        )

    for o in range(1, 8):
        send_force(o).start()
    for side in range(2):
        send_partial(STEPS, side, False).start()

    with jax.named_scope("rg_push"):
        for g in range(3, 9):
            bown[4 * (g - 3) : 4 * (g - 2)] = push_group(g)

    load_prev().wait()

    def finish_term(s, lone):
        for side in range(2):
            n = 1 if lone else 2
            first = (11 - s if lone else 12 - 2 * s) if side == 0 else (12 + s if lone else 10 + 2 * s)
            at = pl.ds(first, n)
            with jax.named_scope("rg_xW"):
                send_partial(s, side, lone).wait_recv()
            both = own[at] + xr[at].astype(F32)
            tno[at] = (2.0 * both - prev[at].astype(F32)).astype(BF)

    def finish_grad(g):
        for side in range(2):
            at = pl.ds(12 * side + 4 * g, 4)
            with jax.named_scope("rg_bW"):
                send_pushed(1 - side, g).wait_recv()
            both = bown[at] + br[side, pl.ds(4 * g, 4)].astype(F32)
            gro[at] = (2.0 * both).astype(BF)

    def finish_loop(s, carry):
        finish_term(s, False)
        return carry

    finish_term(0, True)
    finish_term(1, True)
    finish_grad(0)
    lax.fori_loop(2, STEPS - 1, finish_loop, 0)
    finish_grad(1)
    finish_term(STEPS - 1, False)
    finish_grad(2)
    with jax.named_scope("rg_forceW"):
        for o in range(1, 8):
            take_force(o).wait_recv()
    summed = fbuf[0]
    for s in range(1, 8):
        summed = summed + fbuf[s]
    fo[...] = summed[:, :HALF]
    with jax.named_scope("rg_last"):
        finish_term(STEPS, False)

    with jax.named_scope("rg_tail"):
        for s in range(STEPS + 1):
            to_up(s, s < 2).wait_send()
            to_down(s, s < 2).wait_send()
            for side in range(2):
                send_partial(s, side, s < 2).wait_send()
        for g in range(3):
            for side in range(2):
                send_pushed(side, g).wait_send()
        for o in range(1, 8):
            send_force(o).wait_send()


def write_out(a, b, c, ao, bo, co, sem):
    copies = [
        pltpu.make_async_copy(x, y, sem.at[n])
        for n, (x, y) in enumerate(((a, ao), (b, bo), (c, co)))
    ]
    for copy in copies:
        copy.start()
    for copy in copies:
        copy.wait()


def local(term_now, term_prev, cotangent, ham_blocks, block_mask, ham_slope, atom_owner):
    anyspace = pl.BlockSpec(memory_space=pl.ANY)
    dma = pltpu.SemaphoreType.DMA
    block = (ROWS, HALF, COLS)
    vmem = pl.BlockSpec(memory_space=pltpu.VMEM)
    shapes = ((block, BF), (block, BF), ((ROWS, HALF), F32))
    results = pl.pallas_call(
        kernel,
        out_shape=tuple(pltpu.VMEM(*s) for s in shapes),
        in_specs=[anyspace] * 7,
        out_specs=(vmem, vmem, vmem),
        scratch_shapes=[
            pltpu.SMEM((ROWS, SLOTS), jnp.int32),
            pltpu.VMEM((ROWS, ORB), jnp.int32),
            pltpu.VMEM((ROWS + 2 * REACH, HALF, COLS), BF),
            pltpu.VMEM((24, COLS, ORB), BF),
            pltpu.VMEM((ROWS, ORB, COLS), BF),
            pltpu.VMEM((ROWS, SLOTS, HALF, ORB), BF),
            pltpu.VMEM((ROWS, SLOTS, HALF, ORB), BF),
            pltpu.VMEM(block, F32),
            pltpu.VMEM(block, BF),
            pltpu.VMEM(block, BF),
            pltpu.VMEM(block, F32),
            pltpu.VMEM((2, REACH, HALF, COLS), BF),
            pltpu.VMEM((2, REACH, HALF, COLS), BF),
            pltpu.VMEM(block, BF),
            pltpu.VMEM((ROWS, 1, ORB), F32),
            pltpu.VMEM((8, ROWS, ORB), F32),
            dma((4,)), dma((3,)), dma((2, 2, STEPS)),
            dma((2, STEPS + 1)), dma((2, STEPS + 1)),
            dma((2, STEPS + 1)), dma((2, STEPS + 1)),
            dma((2, 3)), dma((2, 3)),
            dma((7,)), dma((7,)),
        ],
        compiler_params=pltpu.CompilerParams(
            collective_id=0, has_side_effects=True, vmem_limit_bytes=54_000_000
        ),
        name="chebyshev",
    )(block_mask, atom_owner, term_now, term_prev, cotangent, ham_blocks, ham_slope)
    return pl.pallas_call(
        write_out,
        out_shape=tuple(jax.ShapeDtypeStruct(*s) for s in shapes),
        in_specs=[vmem] * 3,
        out_specs=(anyspace,) * 3,
        scratch_shapes=[dma((3,))],
        compiler_params=pltpu.CompilerParams(vmem_limit_bytes=4_000_000),
        name="write_out",
    )(*results)


def solution(mesh):
    return jax.shard_map(
        local,
        mesh=mesh,
        in_specs=(
            P("rows", "layers", "cols"),
            P("rows", "layers", "cols"),
            P("rows", None, "cols"),
            P("rows", None, "layers", None),
            P("rows", None),
            P("rows", None, "layers", None),
            P("rows", None),
        ),
        out_specs=(P("rows", "layers", "cols"), P("rows", "layers", "cols"), P("rows", None)),
        check_vma=False,
    )
```

```python
import jax
import jax.numpy as jnp
from jax import lax
from jax.experimental import pallas as pl
from jax.experimental.pallas import tpu as pltpu
from jax.sharding import PartitionSpec as P

BF = jnp.bfloat16
F32 = jnp.float32
MESH = pl.DeviceIdType.MESH

ROWS = 24
HALF = 64
ORB = 128
COLS = 512
SLOTS = 25
REACH = 12
STEPS = 6
LONE = ((0, 0, 128), (0, 128, 128), (0, 256, 256), (1, 0, 256), (1, 256, 256))
FIRST = len(LONE)
LAST = FIRST + STEPS - 2


def remote(src, dst, send_sem, recv_sem, device):
    return pltpu.make_async_remote_copy(
        src_ref=src, dst_ref=dst, send_sem=send_sem, recv_sem=recv_sem,
        device_id=device, device_id_type=MESH,
    )


def kernel(
    mask_h, owner_h, tn, tp, cot_h, ham_h, slope_h,
    tno, gro, fo,
    mask, owner, ext, tt, cot, ham, slope, own, xs, xr, bown, bs, br, prev, to, go, rf, fbuf, fsum,
    lsem, hsem, osem, hs, hr, xss, xrs, bss, bsr, fs, fr,
):
    row = lax.axis_index("rows")
    col = lax.axis_index("cols")
    lay = lax.axis_index("layers")
    up = {"rows": lax.rem(row + 1, 16)}
    down = {"rows": lax.rem(row + 15, 16)}
    partner = {"layers": 1 - lay}
    me = col * 2 + lay

    def ring(index):
        return {"cols": index // 2, "layers": index % 2}

    def load_term():
        return pltpu.make_async_copy(tn, ext.at[pl.ds(REACH, ROWS)], lsem.at[0])

    def load_mask():
        return pltpu.make_async_copy(mask_h, mask, lsem.at[2])

    def load_owner():
        return pltpu.make_async_copy(owner_h, owner, lsem.at[3])

    load_term().start()
    barrier = pltpu.get_barrier_semaphore()
    pl.semaphore_signal(barrier, 1, device_id=up, device_id_type=MESH)
    pl.semaphore_signal(barrier, 1, device_id=down, device_id_type=MESH)
    for o in range(1, 8):
        pl.semaphore_signal(
            barrier, 1, device_id=ring(lax.rem(me + o, 8)), device_id_type=MESH
        )

    def load_cot(part):
        at = (pl.ds(10, 4), pl.ds(0, 10), pl.ds(14, 10))[part]
        return pltpu.make_async_copy(cot_h.at[at], cot.at[at], lsem.at[4 if part else 5])

    def cot_rest():
        return pltpu.make_async_copy(
            cot_h.at[pl.ds(0, 20)], cot.at[pl.ds(0, 20)], lsem.at[4]
        )

    def load_prev():
        return pltpu.make_async_copy(tp, prev, lsem.at[1])

    def load_blocks(k):
        copies = []
        for first in (10 - 2 * k, 12 + 2 * k):
            at = pl.ds(first, 2)
            copies.append(pltpu.make_async_copy(ham_h.at[at], ham.at[at], hsem.at[k]))
            copies.append(pltpu.make_async_copy(slope_h.at[at], slope.at[at], hsem.at[k]))
        return copies

    def have_blocks(k):
        at = pl.ds(0, 8)
        pltpu.make_async_copy(ham_h.at[at], ham.at[at], hsem.at[k]).wait()

    load_mask().start()
    for c in load_blocks(0):
        c.start()
    load_cot(0).start()

    def to_up(s):
        return remote(
            ext.at[pl.ds(42 - 2 * s, 2)], ext.at[pl.ds(18 - 2 * s, 2)],
            hs.at[0], hr.at[s], up,
        )

    def to_down(s):
        return remote(
            ext.at[pl.ds(4 + 2 * s, 2)], ext.at[pl.ds(28 + 2 * s, 2)],
            hs.at[0], hr.at[s], down,
        )

    def lone_up(u):
        away, c0, n = LONE[u]
        cs = pl.ds(c0, n)
        return remote(
            ext.at[pl.ds(35 - away, 1), :, cs], ext.at[pl.ds(11 - away, 1), :, cs],
            hs.at[0], hr.at[u], up,
        )

    def lone_down(u):
        away, c0, n = LONE[u]
        cs = pl.ds(c0, n)
        return remote(
            ext.at[pl.ds(12 + away, 1), :, cs], ext.at[pl.ds(36 + away, 1), :, cs],
            hs.at[0], hr.at[u], down,
        )

    def halo_bytes(rows, cs, sem):
        at = pl.ds(REACH, rows), slice(None), cs
        return remote(ext.at[at], ext.at[at], hs.at[0], sem, up)

    def have_lone(u):
        halo_bytes(2, pl.ds(LONE[u][1], LONE[u][2]), hr.at[u]).wait_recv()

    def have_halo(s):
        halo_bytes(4, pl.ds(0, COLS), hr.at[s]).wait_recv()

    def start_lone(u):
        lone_up(u).start()
        lone_down(u).start()

    def start_halo(s):
        to_up(s).start()
        to_down(s).start()

    with jax.named_scope("rg_term"):
        load_term().wait()
    with jax.named_scope("rg_barrier"):
        pl.semaphore_wait(barrier, 9)
    for u in range(3):
        start_lone(u)

    def turn(pair):
        tt[pair] = ext[pl.ds(2 * pair, 2)].reshape(ORB, COLS).T

    def turn_local(p, carry):
        turn(p + 6)
        return carry

    lax.fori_loop(0, 6, turn_local, 0)
    start_lone(3)
    for c in load_blocks(1):
        c.start()
    lax.fori_loop(6, 12, turn_local, 0)
    start_lone(4)
    load_cot(1).start()
    load_cot(2).start()

    def mask_rows(k, carry):
        have_blocks(k)
        for first in (10 - 2 * k, 12 + 2 * k):
            for r in range(2):
                i = first + r
                for d in range(SLOTS):
                    kept = jnp.full((HALF, ORB), mask[i, d].astype(F32), F32).astype(BF)
                    ham[i, d] = ham[i, d] * kept
                    slope[i, d] = slope[i, d] * kept
        return carry

    def step_rows(s, side):
        return 18 - 2 * s if side == 0 else 4 + 2 * s

    def send_partial(s, side):
        at = pl.ds(step_rows(s, side), 2)
        return remote(
            xs.at[at], xr.at[at], xss.at[0], xrs.at[s], partner
        )

    def lone_at(u, side):
        away, c0, n = LONE[u]
        return pl.ds(12 + away if side else 11 - away, 1), slice(None), pl.ds(c0, n)

    def send_lone(u, side):
        at = lone_at(u, side)
        return remote(
            xs.at[at], xr.at[at], xss.at[0], xrs.at[u], partner
        )

    def stacked(i, before, after):
        w = jnp.concatenate(
            [ham[i].reshape(SLOTS * HALF, ORB), slope[i].reshape(SLOTS * HALF, ORB)],
            axis=1,
        )
        parts = [w]
        if before:
            parts = [jnp.zeros((HALF * before, 2 * ORB), BF)] + parts
        if after:
            parts = parts + [jnp.zeros((HALF * after, 2 * ORB), BF)]
        return jnp.concatenate(parts, axis=0)

    def product(pair, pairs, rows, c0=0, cols=COLS):
        cs = slice(c0, c0 + cols)
        lhs = jnp.concatenate([tt[pair + g, cs] for g in range(pairs)], axis=1)
        weights = [stacked(i, r, 2 * pairs - SLOTS - r) for i, r in rows]
        out = jnp.dot(lhs, jnp.concatenate(weights, axis=1), preferred_element_type=F32)
        for n, (i, _) in enumerate(rows):
            f = out[:, 2 * n * ORB : (2 * n + 1) * ORB].T
            low, high = f[:HALF], f[HALF:]
            own[i, :, cs] = jnp.where(lay == 0, low, high)
            xs[i, :, cs] = jnp.where(lay == 0, high, low).astype(BF)
            g = out[:, (2 * n + 1) * ORB : (2 * n + 2) * ORB]
            turned = cot[i, :, cs].T.astype(F32)
            part = 2.0 * jnp.sum(turned * g, axis=0, keepdims=True)
            rf[i] = rf[i] + part if c0 else part

    nothing = jnp.zeros((HALF, COLS), BF)

    def forward_lone(u):
        away, c0, n = LONE[u]
        cs = slice(c0, c0 + n)
        with jax.named_scope("rg_halo"):
            have_lone(u)
        low = jnp.concatenate([ext[10, :, cs] if away else nothing[:, :n], ext[11, :, cs]], axis=0)
        high = jnp.concatenate([ext[36, :, cs], ext[37, :, cs] if away else nothing[:, :n]], axis=0)
        tt[5, cs] = low.T
        tt[18, cs] = high.T
        product(5, 14, ((10, 0), (13, 3)) if away else ((11, 1), (12, 2)), c0, n)
        for side in range(2):
            send_lone(u, side).start()

    def forward(s, carry):
        with jax.named_scope("rg_halo"):
            have_halo(s)
        turn(9 - s)
        turn(14 + s)
        for side in range(2):
            pair = 9 - s if side == 0 else 2 + s
            product(pair, 13, ((2 * pair, 0), (2 * pair + 1, 1)))

            @pl.when(s < LAST)
            def _():
                send_partial(s, side).start()

        return carry

    def push_group(g):
        i0, i1 = max(0, 4 * g - 24), min(ROWS - 1, 4 * g + 3)
        parts = []
        for i in range(i0, i1 + 1):
            d0 = 4 * g - i
            lo, hi = max(0, -d0), min(4, SLOTS - d0)
            p = []
            if lo:
                p.append(jnp.zeros((HALF * lo, ORB), BF))
            p.append(ham[i, d0 + lo : d0 + hi].reshape((hi - lo) * HALF, ORB))
            if hi < 4:
                p.append(jnp.zeros((HALF * (4 - hi), ORB), BF))
            parts.append(jnp.concatenate(p, axis=0) if len(p) > 1 else p[0])
        out = jnp.dot(
            jnp.concatenate(parts, axis=1),
            cot[i0 : i1 + 1].reshape((i1 - i0 + 1) * ORB, COLS),
            preferred_element_type=F32,
        )
        return out.reshape(4, HALF, COLS)

    def send_pushed(side, g):
        at = pl.ds(4 * g, 4)
        return remote(
            bs.at[side, at], br.at[1 - side, at], bss.at[0], bsr.at[g],
            down if side == 0 else up,
        )

    with jax.named_scope("rg_mask0"):
        load_mask().wait()
        mask_rows(0, 0)
    load_cot(0).wait()
    start_halo(5)
    for k in range(2, STEPS):
        for c in load_blocks(k):
            c.start()
    load_prev().start()
    load_owner().start()
    with jax.named_scope("rg_fwd0"):
        for u in range(3):
            forward_lone(u)
    start_halo(6)
    with jax.named_scope("rg_fwd1"):
        for u in range(3, 5):
            forward_lone(u)
    start_halo(7)
    with jax.named_scope("rg_mask1"):
        cot_rest().wait()
        mask_rows(1, 0)
    start_halo(8)
    with jax.named_scope("rg_fwd2"):
        forward(FIRST, 0)
    start_halo(9)
    with jax.named_scope("rg_fwd3"):
        mask_rows(2, 0)
        forward(FIRST + 1, 0)
    with jax.named_scope("rg_mask2"):
        lax.fori_loop(3, STEPS, mask_rows, 0)
    with jax.named_scope("rg_edges"):
        for g in range(3):
            bs[0, 4 * g : 4 * g + 4] = push_group(g).astype(BF)
            bs[1, 4 * g : 4 * g + 4] = push_group(9 + g).astype(BF)
            send_pushed(0, g).start()
            send_pushed(1, g).start()
    with jax.named_scope("rg_fwd"):
        lax.fori_loop(FIRST + 2, LAST + 1, forward, 0)
    load_owner().wait()

    atoms = lax.broadcasted_iota(jnp.int32, (HALF, ORB), 0)
    lanes = lax.broadcasted_iota(jnp.int32, (HALF, ORB), 1)

    def gather_atoms(i, total):
        mine = jnp.where(owner[pl.ds(i, 1)] == atoms, rf[i], 0.0)
        summed = jnp.sum(mine, axis=1, keepdims=True)
        return total + jnp.where(lanes == i, summed, 0.0)

    total = lax.fori_loop(0, ROWS, gather_atoms, jnp.zeros((HALF, ORB), F32))
    total = jnp.concatenate([total, jnp.zeros((HALF, ORB), F32)], axis=0).T
    fbuf[me] = total[:ROWS]

    def send_force(o):
        return remote(
            fbuf.at[me], fbuf.at[me], fs.at[0], fr.at[0],
            ring(lax.rem(me + o, 8)),
        )

    def all_forces():
        at = pl.ds(0, 7)
        return remote(fbuf.at[at], fbuf.at[at], fs.at[0], fr.at[0], partner)

    for o in range(1, 8):
        send_force(o).start()
    for side in range(2):
        send_partial(LAST, side).start()

    with jax.named_scope("rg_push"):
        for g in range(3, 9):
            bown[4 * (g - 3) : 4 * (g - 2)] = push_group(g)

    load_prev().wait()

    def out_term(s, side):
        at = pl.ds(step_rows(s, side), 2)
        return pltpu.make_async_copy(to.at[at], tno.at[at], osem.at[0])

    def out_middle():
        at = pl.ds(10, 4)
        return pltpu.make_async_copy(to.at[at], tno.at[at], osem.at[0])

    def out_grad(side, g):
        at = pl.ds(12 * side + 4 * g, 4)
        return pltpu.make_async_copy(go.at[at], gro.at[at], osem.at[1])

    def finish_at(at):
        both = own[at] + xr[at].astype(F32)
        to[at] = (2.0 * both - prev[at].astype(F32)).astype(BF)

    def have_partial(s, rows, cs):
        at = pl.ds(0, rows), slice(None), cs
        with jax.named_scope("rg_xW"):
            remote(xs.at[at], xr.at[at], xss.at[0], xrs.at[s], partner).wait_recv()

    def finish_term(s, carry):
        have_partial(s, 4, pl.ds(0, COLS))
        for side in range(2):
            finish_at(pl.ds(step_rows(s, side), 2))
            out_term(s, side).start()
        return carry

    def have_pushed(g):
        at = pl.ds(4 * g, 4)
        remote(bs.at[:, at], br.at[:, at], bss.at[0], bsr.at[g], up).wait_recv()

    def finish_grad(g):
        with jax.named_scope("rg_bW"):
            have_pushed(g)
        for side in range(2):
            at = pl.ds(12 * side + 4 * g, 4)
            both = bown[at] + br[side, pl.ds(4 * g, 4)].astype(F32)
            go[at] = (2.0 * both).astype(BF)
            out_grad(side, g).start()

    for u in range(FIRST):
        have_partial(u, 2, pl.ds(LONE[u][1], LONE[u][2]))
    finish_at(pl.ds(10, 4))
    out_middle().start()
    finish_grad(0)
    lax.fori_loop(FIRST, LAST - 1, finish_term, 0)
    finish_grad(1)
    finish_term(LAST - 1, 0)
    finish_grad(2)
    with jax.named_scope("rg_forceW"):
        all_forces().wait_recv()
    summed = fbuf[0]
    for s in range(1, 8):
        summed = summed + fbuf[s]
    fsum[...] = summed[:, :HALF]
    force_out = pltpu.make_async_copy(fsum, fo, osem.at[2])
    force_out.start()

    with jax.named_scope("rg_sent"):
        sent = ext.at[pl.ds(0, ROWS)]
        remote(sent, sent, hs.at[0], hr.at[0], up).wait_send()
        remote(bs, br, bss.at[0], bsr.at[0], up).wait_send()
        all_forces().wait_send()
        force_out.wait()
        pltpu.make_async_copy(go, gro, osem.at[1]).wait()
    with jax.named_scope("rg_last"):
        finish_term(LAST, 0)
    with jax.named_scope("rg_tail"):
        remote(xs, xr, xss.at[0], xrs.at[0], partner).wait_send()
        pltpu.make_async_copy(to, tno, osem.at[0]).wait()


def write_out(a, b, c, ao, bo, co, sem):
    copies = [pltpu.make_async_copy(c, co, sem.at[0])]
    for n, (x, y) in enumerate(((a, ao), (b, bo))):
        for part in range(4):
            at = pl.ds(6 * part, 6)
            copies.append(pltpu.make_async_copy(x.at[at], y.at[at], sem.at[1 + 4 * n + part]))
    for copy in copies:
        copy.start()
    for copy in copies:
        copy.wait()


def local(term_now, term_prev, cotangent, ham_blocks, block_mask, ham_slope, atom_owner):
    anyspace = pl.BlockSpec(memory_space=pl.ANY)
    dma = pltpu.SemaphoreType.DMA
    block = (ROWS, HALF, COLS)
    shapes = ((block, BF), (block, BF), ((ROWS, HALF), F32))
    results = pl.pallas_call(
        kernel,
        out_shape=tuple(pltpu.VMEM(*s) for s in shapes),
        in_specs=[anyspace] * 7,
        out_specs=(anyspace,) * 3,
        scratch_shapes=[
            pltpu.SMEM((ROWS, SLOTS), jnp.int32),
            pltpu.VMEM((ROWS, ORB), jnp.int32),
            pltpu.VMEM((ROWS + 2 * REACH, HALF, COLS), BF),
            pltpu.VMEM((24, COLS, ORB), BF),
            pltpu.VMEM((ROWS, ORB, COLS), BF),
            pltpu.VMEM((ROWS, SLOTS, HALF, ORB), BF),
            pltpu.VMEM((ROWS, SLOTS, HALF, ORB), BF),
            pltpu.VMEM(block, F32),
            pltpu.VMEM(block, BF),
            pltpu.VMEM(block, BF),
            pltpu.VMEM(block, F32),
            pltpu.VMEM((2, REACH, HALF, COLS), BF),
            pltpu.VMEM((2, REACH, HALF, COLS), BF),
            pltpu.VMEM(block, BF),
            pltpu.VMEM(block, BF),
            pltpu.VMEM(block, BF),
            pltpu.VMEM((ROWS, 1, ORB), F32),
            pltpu.VMEM((8, ROWS, ORB), F32),
            pltpu.VMEM((ROWS, HALF), F32),
            dma((6,)), dma((STEPS,)), dma((3,)),
            dma((1,)), dma((LAST + 1,)),
            dma((1,)), dma((LAST + 1,)),
            dma((1,)), dma((3,)),
            dma((1,)), dma((1,)),
        ],
        compiler_params=pltpu.CompilerParams(
            collective_id=0, has_side_effects=True, vmem_limit_bytes=54_000_000
        ),
        name="chebyshev",
    )(block_mask, atom_owner, term_now, term_prev, cotangent, ham_blocks, ham_slope)
    return pl.pallas_call(
        write_out,
        out_shape=tuple(jax.ShapeDtypeStruct(*s) for s in shapes),
        in_specs=[anyspace] * 3,
        out_specs=(anyspace,) * 3,
        scratch_shapes=[dma((9,))],
        compiler_params=pltpu.CompilerParams(vmem_limit_bytes=4_000_000),
        name="write_out",
    )(*results)


def solution(mesh):
    return jax.shard_map(
        local,
        mesh=mesh,
        in_specs=(
            P("rows", "layers", "cols"),
            P("rows", "layers", "cols"),
            P("rows", None, "cols"),
            P("rows", None, "layers", None),
            P("rows", None),
            P("rows", None, "layers", None),
            P("rows", None),
        ),
        out_specs=(P("rows", "layers", "cols"), P("rows", "layers", "cols"), P("rows", None)),
        check_vma=False,
    )
```

```python
import jax
import jax.numpy as jnp
from jax import lax
from jax.experimental import pallas as pl
from jax.experimental.pallas import tpu as pltpu
from jax.sharding import PartitionSpec as P

BF = jnp.bfloat16
F32 = jnp.float32
MESH = pl.DeviceIdType.MESH

ROWS = 24
HALF = 64
ORB = 128
COLS = 512
SLOTS = 25
REACH = 12
STEPS = 6
LONE = ((0, 0, 128), (0, 128, 128), (0, 256, 256), (1, 0, 256), (1, 256, 256))
FIRST = len(LONE)
LAST = FIRST + STEPS - 2


def remote(src, dst, send_sem, recv_sem, device):
    return pltpu.make_async_remote_copy(
        src_ref=src, dst_ref=dst, send_sem=send_sem, recv_sem=recv_sem,
        device_id=device, device_id_type=MESH,
    )


def kernel(
    mask_h, owner_h, tn, tp, cot_h, ham_h, slope_h,
    tno, gro, fo,
    mask, owner, ext, tt, cot, ham, slope, own, xs, xr, bown, bs, br, prev, to, go, rf, fpart, fbuf, fsum,
    lsem, hsem, osem, hs, hr, xss, xrs, bss, bsr, fs, fr,
):
    row = lax.axis_index("rows")
    col = lax.axis_index("cols")
    lay = lax.axis_index("layers")
    up = {"rows": lax.rem(row + 1, 16)}
    down = {"rows": lax.rem(row + 15, 16)}
    partner = {"layers": 1 - lay}
    core = lax.rem(col, 2)
    chip = lay * 2 + lax.div(col, 2)
    mate = {"cols": col + 1 - 2 * core}

    def ring(o):
        other = lax.rem(chip + o, 4)
        return {"cols": lax.rem(other, 2) * 2 + core, "layers": lax.div(other, 2)}

    def load_term():
        return pltpu.make_async_copy(tn, ext.at[pl.ds(REACH, ROWS)], lsem.at[0])

    def load_mask():
        return pltpu.make_async_copy(mask_h, mask, lsem.at[2])

    def load_owner():
        return pltpu.make_async_copy(owner_h, owner, lsem.at[3])

    load_term().start()
    barrier = pltpu.get_barrier_semaphore()
    pl.semaphore_signal(barrier, 1, device_id=up, device_id_type=MESH)
    pl.semaphore_signal(barrier, 1, device_id=down, device_id_type=MESH)
    pl.semaphore_signal(barrier, 1, device_id=mate, device_id_type=MESH)
    for o in range(1, 4):
        pl.semaphore_signal(barrier, 1, device_id=ring(o), device_id_type=MESH)

    def load_cot(part):
        at = (pl.ds(10, 4), pl.ds(0, 10), pl.ds(14, 10))[part]
        return pltpu.make_async_copy(cot_h.at[at], cot.at[at], lsem.at[4 if part else 5])

    def cot_rest():
        return pltpu.make_async_copy(
            cot_h.at[pl.ds(0, 20)], cot.at[pl.ds(0, 20)], lsem.at[4]
        )

    def load_prev():
        return pltpu.make_async_copy(tp, prev, lsem.at[1])

    def load_blocks(k):
        copies = []
        for first in (10 - 2 * k, 12 + 2 * k):
            at = pl.ds(first, 2)
            copies.append(pltpu.make_async_copy(ham_h.at[at], ham.at[at], hsem.at[k]))
            copies.append(pltpu.make_async_copy(slope_h.at[at], slope.at[at], hsem.at[k]))
        return copies

    def have_blocks(k):
        at = pl.ds(0, 8)
        pltpu.make_async_copy(ham_h.at[at], ham.at[at], hsem.at[k]).wait()

    load_mask().start()
    for c in load_blocks(0):
        c.start()
    load_cot(0).start()

    def to_up(s):
        return remote(
            ext.at[pl.ds(42 - 2 * s, 2)], ext.at[pl.ds(18 - 2 * s, 2)],
            hs.at[0], hr.at[s], up,
        )

    def to_down(s):
        return remote(
            ext.at[pl.ds(4 + 2 * s, 2)], ext.at[pl.ds(28 + 2 * s, 2)],
            hs.at[0], hr.at[s], down,
        )

    def lone_up(u):
        away, c0, n = LONE[u]
        cs = pl.ds(c0, n)
        return remote(
            ext.at[pl.ds(35 - away, 1), :, cs], ext.at[pl.ds(11 - away, 1), :, cs],
            hs.at[0], hr.at[u], up,
        )

    def lone_down(u):
        away, c0, n = LONE[u]
        cs = pl.ds(c0, n)
        return remote(
            ext.at[pl.ds(12 + away, 1), :, cs], ext.at[pl.ds(36 + away, 1), :, cs],
            hs.at[0], hr.at[u], down,
        )

    def halo_bytes(rows, cs, sem):
        at = pl.ds(REACH, rows), slice(None), cs
        return remote(ext.at[at], ext.at[at], hs.at[0], sem, up)

    def have_lone(u):
        halo_bytes(2, pl.ds(LONE[u][1], LONE[u][2]), hr.at[u]).wait_recv()

    def have_halo(s):
        halo_bytes(4, pl.ds(0, COLS), hr.at[s]).wait_recv()

    def start_lone(u):
        lone_up(u).start()
        lone_down(u).start()

    def start_halo(s):
        to_up(s).start()
        to_down(s).start()

    with jax.named_scope("rg_term"):
        load_term().wait()
    with jax.named_scope("rg_barrier"):
        pl.semaphore_wait(barrier, 6)
    start_lone(0)

    def turn(pair):
        tt[pair] = ext[pl.ds(2 * pair, 2)].reshape(ORB, COLS).T

    def turn_local(p, carry):
        turn(p + 6)
        return carry

    for u in range(1, 4):
        lax.fori_loop(4 * u - 4, 4 * u, turn_local, 0)
        start_lone(u)
    for c in load_blocks(1):
        c.start()

    def mask_rows(k, carry):
        have_blocks(k)
        for first in (10 - 2 * k, 12 + 2 * k):
            for r in range(2):
                i = first + r
                for d in range(SLOTS):
                    kept = jnp.full((HALF, ORB), mask[i, d].astype(F32), F32).astype(BF)
                    ham[i, d] = ham[i, d] * kept
                    slope[i, d] = slope[i, d] * kept
        return carry

    def step_rows(s, side):
        return 18 - 2 * s if side == 0 else 4 + 2 * s

    def send_partial(s, side):
        at = pl.ds(step_rows(s, side), 2)
        return remote(
            xs.at[at], xr.at[at], xss.at[0], xrs.at[s], partner
        )

    def lone_at(u, side):
        away, c0, n = LONE[u]
        return pl.ds(12 + away if side else 11 - away, 1), slice(None), pl.ds(c0, n)

    def send_lone(u, side):
        at = lone_at(u, side)
        return remote(
            xs.at[at], xr.at[at], xss.at[0], xrs.at[u], partner
        )

    def stacked(i, before, after):
        w = jnp.concatenate(
            [ham[i].reshape(SLOTS * HALF, ORB), slope[i].reshape(SLOTS * HALF, ORB)],
            axis=1,
        )
        parts = [w]
        if before:
            parts = [jnp.zeros((HALF * before, 2 * ORB), BF)] + parts
        if after:
            parts = parts + [jnp.zeros((HALF * after, 2 * ORB), BF)]
        return jnp.concatenate(parts, axis=0)

    def product(pair, pairs, rows, c0=0, cols=COLS):
        cs = slice(c0, c0 + cols)
        lhs = jnp.concatenate([tt[pair + g, cs] for g in range(pairs)], axis=1)
        weights = [stacked(i, r, 2 * pairs - SLOTS - r) for i, r in rows]
        out = jnp.dot(lhs, jnp.concatenate(weights, axis=1), preferred_element_type=F32)
        for n, (i, _) in enumerate(rows):
            f = out[:, 2 * n * ORB : (2 * n + 1) * ORB].T
            low, high = f[:HALF], f[HALF:]
            own[i, :, cs] = jnp.where(lay == 0, low, high)
            xs[i, :, cs] = jnp.where(lay == 0, high, low).astype(BF)
            g = out[:, (2 * n + 1) * ORB : (2 * n + 2) * ORB]
            turned = cot[i, :, cs].T.astype(F32)
            part = 2.0 * jnp.sum(turned * g, axis=0, keepdims=True)
            rf[i] = rf[i] + part if c0 else part

    nothing = jnp.zeros((HALF, COLS), BF)

    def forward_lone(u):
        away, c0, n = LONE[u]
        cs = slice(c0, c0 + n)
        with jax.named_scope("rg_halo"):
            have_lone(u)
        low = jnp.concatenate([ext[10, :, cs] if away else nothing[:, :n], ext[11, :, cs]], axis=0)
        high = jnp.concatenate([ext[36, :, cs], ext[37, :, cs] if away else nothing[:, :n]], axis=0)
        tt[5, cs] = low.T
        tt[18, cs] = high.T
        product(5, 14, ((10, 0), (13, 3)) if away else ((11, 1), (12, 2)), c0, n)
        for side in range(2):
            send_lone(u, side).start()

    def forward(s, carry):
        with jax.named_scope("rg_halo"):
            have_halo(s)
        turn(9 - s)
        turn(14 + s)
        for side in range(2):
            pair = 9 - s if side == 0 else 2 + s
            product(pair, 13, ((2 * pair, 0), (2 * pair + 1, 1)))

            @pl.when(s < LAST)
            def _():
                send_partial(s, side).start()

        return carry

    def push_group(g):
        i0, i1 = max(0, 4 * g - 24), min(ROWS - 1, 4 * g + 3)
        parts = []
        for i in range(i0, i1 + 1):
            d0 = 4 * g - i
            lo, hi = max(0, -d0), min(4, SLOTS - d0)
            p = []
            if lo:
                p.append(jnp.zeros((HALF * lo, ORB), BF))
            p.append(ham[i, d0 + lo : d0 + hi].reshape((hi - lo) * HALF, ORB))
            if hi < 4:
                p.append(jnp.zeros((HALF * (4 - hi), ORB), BF))
            parts.append(jnp.concatenate(p, axis=0) if len(p) > 1 else p[0])
        out = jnp.dot(
            jnp.concatenate(parts, axis=1),
            cot[i0 : i1 + 1].reshape((i1 - i0 + 1) * ORB, COLS),
            preferred_element_type=F32,
        )
        return out.reshape(4, HALF, COLS)

    def send_pushed(side, g):
        at = pl.ds(4 * g, 4)
        return remote(
            bs.at[side, at], br.at[1 - side, at], bss.at[0], bsr.at[g],
            down if side == 0 else up,
        )

    with jax.named_scope("rg_mask0"):
        load_mask().wait()
        mask_rows(0, 0)
    start_lone(4)
    load_cot(1).start()
    load_cot(2).start()
    start_halo(5)
    for k in range(2, STEPS):
        for c in load_blocks(k):
            c.start()
    load_prev().start()
    load_owner().start()
    load_cot(0).wait()
    with jax.named_scope("rg_fwd0"):
        for u in range(3):
            forward_lone(u)
    start_halo(6)
    with jax.named_scope("rg_fwd1"):
        for u in range(3, 5):
            forward_lone(u)
    start_halo(7)
    with jax.named_scope("rg_mask1"):
        cot_rest().wait()
        mask_rows(1, 0)
    start_halo(8)
    with jax.named_scope("rg_fwd2"):
        forward(FIRST, 0)
    start_halo(9)
    with jax.named_scope("rg_fwd3"):
        mask_rows(2, 0)
        forward(FIRST + 1, 0)
    with jax.named_scope("rg_mask2"):
        lax.fori_loop(3, STEPS, mask_rows, 0)
    with jax.named_scope("rg_edges"):
        for g in range(3):
            bs[0, 4 * g : 4 * g + 4] = push_group(g).astype(BF)
            bs[1, 4 * g : 4 * g + 4] = push_group(9 + g).astype(BF)
            send_pushed(0, g).start()
            send_pushed(1, g).start()
    with jax.named_scope("rg_fwd"):
        lax.fori_loop(FIRST + 2, LAST + 1, forward, 0)
    load_owner().wait()

    atoms = lax.broadcasted_iota(jnp.int32, (HALF, ORB), 0)
    lanes = lax.broadcasted_iota(jnp.int32, (HALF, ORB), 1)

    def gather_atoms(i, totals):
        both = []
        for total, j in zip(totals, (i, i + 12)):
            mine = jnp.where(owner[pl.ds(j, 1)] == atoms, rf[j], 0.0)
            summed = jnp.sum(mine, axis=1, keepdims=True)
            both.append(total + jnp.where(lanes == i, summed, 0.0))
        return tuple(both)

    zero = jnp.zeros((HALF, ORB), F32)
    totals = lax.fori_loop(0, 12, gather_atoms, (zero, zero))
    fpart[0] = jnp.concatenate(totals, axis=0).T[:16]

    def to_mate():
        return remote(fpart.at[0], fpart.at[1], fs.at[0], fr.at[0], mate)

    def send_force(o):
        return remote(fbuf.at[chip], fbuf.at[chip], fs.at[1], fr.at[1], ring(o))

    def all_forces():
        at = pl.ds(0, 3)
        return remote(fbuf.at[at], fbuf.at[at], fs.at[1], fr.at[1], partner)

    to_mate().start()
    with jax.named_scope("rg_push"):
        bown[0:4] = push_group(3)
    to_mate().wait()
    fbuf[chip] = fpart[0] + fpart[1]
    for o in range(1, 4):
        send_force(o).start()
    for side in range(2):
        send_partial(LAST, side).start()

    with jax.named_scope("rg_push"):
        for g in range(4, 9):
            bown[4 * (g - 3) : 4 * (g - 2)] = push_group(g)

    load_prev().wait()

    def out_term(s, side):
        at = pl.ds(step_rows(s, side), 2)
        return pltpu.make_async_copy(to.at[at], tno.at[at], osem.at[0])

    def out_middle():
        at = pl.ds(10, 4)
        return pltpu.make_async_copy(to.at[at], tno.at[at], osem.at[0])

    def out_grad(side, g):
        at = pl.ds(12 * side + 4 * g, 4)
        return pltpu.make_async_copy(go.at[at], gro.at[at], osem.at[1])

    def finish_at(at):
        both = own[at] + xr[at].astype(F32)
        to[at] = (2.0 * both - prev[at].astype(F32)).astype(BF)

    def have_partial(s, rows, cs):
        at = pl.ds(0, rows), slice(None), cs
        with jax.named_scope("rg_xW"):
            remote(xs.at[at], xr.at[at], xss.at[0], xrs.at[s], partner).wait_recv()

    def finish_term(s, carry):
        have_partial(s, 4, pl.ds(0, COLS))
        for side in range(2):
            finish_at(pl.ds(step_rows(s, side), 2))
            out_term(s, side).start()
        return carry

    def have_pushed(g):
        at = pl.ds(4 * g, 4)
        remote(bs.at[:, at], br.at[:, at], bss.at[0], bsr.at[g], up).wait_recv()

    def finish_grad(g):
        with jax.named_scope("rg_bW"):
            have_pushed(g)
        for side in range(2):
            at = pl.ds(12 * side + 4 * g, 4)
            both = bown[at] + br[side, pl.ds(4 * g, 4)].astype(F32)
            go[at] = (2.0 * both).astype(BF)
            out_grad(side, g).start()

    for u in range(FIRST):
        have_partial(u, 2, pl.ds(LONE[u][1], LONE[u][2]))
    finish_at(pl.ds(10, 4))
    out_middle().start()
    finish_grad(0)
    lax.fori_loop(FIRST, LAST - 1, finish_term, 0)
    finish_grad(1)
    finish_term(LAST - 1, 0)
    finish_grad(2)
    with jax.named_scope("rg_forceW"):
        all_forces().wait_recv()
    summed = fbuf[0]
    for s in range(1, 4):
        summed = summed + fbuf[s]
    fsum[0:12] = summed[:12, :HALF]
    fsum[12:24] = summed[:12, HALF:]
    force_out = pltpu.make_async_copy(fsum, fo, osem.at[2])
    force_out.start()

    with jax.named_scope("rg_sent"):
        sent = ext.at[pl.ds(0, ROWS)]
        remote(sent, sent, hs.at[0], hr.at[0], up).wait_send()
        remote(bs, br, bss.at[0], bsr.at[0], up).wait_send()
        all_forces().wait_send()
        force_out.wait()
        pltpu.make_async_copy(go, gro, osem.at[1]).wait()
    with jax.named_scope("rg_last"):
        finish_term(LAST, 0)
    with jax.named_scope("rg_tail"):
        remote(xs, xr, xss.at[0], xrs.at[0], partner).wait_send()
        pltpu.make_async_copy(to, tno, osem.at[0]).wait()


def write_out(a, b, c, ao, bo, co, sem):
    copies = [pltpu.make_async_copy(c, co, sem.at[0])]
    for n, (x, y) in enumerate(((a, ao), (b, bo))):
        for part in range(4):
            at = pl.ds(6 * part, 6)
            copies.append(pltpu.make_async_copy(x.at[at], y.at[at], sem.at[1 + 4 * n + part]))
    for copy in copies:
        copy.start()
    for copy in copies:
        copy.wait()


def local(term_now, term_prev, cotangent, ham_blocks, block_mask, ham_slope, atom_owner):
    anyspace = pl.BlockSpec(memory_space=pl.ANY)
    dma = pltpu.SemaphoreType.DMA
    block = (ROWS, HALF, COLS)
    shapes = ((block, BF), (block, BF), ((ROWS, HALF), F32))
    results = pl.pallas_call(
        kernel,
        out_shape=tuple(pltpu.VMEM(*s) for s in shapes),
        in_specs=[anyspace] * 7,
        out_specs=(anyspace,) * 3,
        scratch_shapes=[
            pltpu.SMEM((ROWS, SLOTS), jnp.int32),
            pltpu.VMEM((ROWS, ORB), jnp.int32),
            pltpu.VMEM((ROWS + 2 * REACH, HALF, COLS), BF),
            pltpu.VMEM((24, COLS, ORB), BF),
            pltpu.VMEM((ROWS, ORB, COLS), BF),
            pltpu.VMEM((ROWS, SLOTS, HALF, ORB), BF),
            pltpu.VMEM((ROWS, SLOTS, HALF, ORB), BF),
            pltpu.VMEM(block, F32),
            pltpu.VMEM(block, BF),
            pltpu.VMEM(block, BF),
            pltpu.VMEM(block, F32),
            pltpu.VMEM((2, REACH, HALF, COLS), BF),
            pltpu.VMEM((2, REACH, HALF, COLS), BF),
            pltpu.VMEM(block, BF),
            pltpu.VMEM(block, BF),
            pltpu.VMEM(block, BF),
            pltpu.VMEM((ROWS, 1, ORB), F32),
            pltpu.VMEM((2, 16, ORB), F32),
            pltpu.VMEM((4, 16, ORB), F32),
            pltpu.VMEM((ROWS, HALF), F32),
            dma((6,)), dma((STEPS,)), dma((3,)),
            dma((1,)), dma((LAST + 1,)),
            dma((1,)), dma((LAST + 1,)),
            dma((1,)), dma((3,)),
            dma((2,)), dma((2,)),
        ],
        compiler_params=pltpu.CompilerParams(
            collective_id=0, has_side_effects=True, vmem_limit_bytes=54_000_000
        ),
        name="chebyshev",
    )(block_mask, atom_owner, term_now, term_prev, cotangent, ham_blocks, ham_slope)
    return pl.pallas_call(
        write_out,
        out_shape=tuple(jax.ShapeDtypeStruct(*s) for s in shapes),
        in_specs=[anyspace] * 3,
        out_specs=(anyspace,) * 3,
        scratch_shapes=[dma((9,))],
        compiler_params=pltpu.CompilerParams(vmem_limit_bytes=4_000_000),
        name="write_out",
    )(*results)


def solution(mesh):
    return jax.shard_map(
        local,
        mesh=mesh,
        in_specs=(
            P("rows", "layers", "cols"),
            P("rows", "layers", "cols"),
            P("rows", None, "cols"),
            P("rows", None, "layers", None),
            P("rows", None),
            P("rows", None, "layers", None),
            P("rows", None),
        ),
        out_specs=(P("rows", "layers", "cols"), P("rows", "layers", "cols"), P("rows", None)),
        check_vma=False,
    )
```

```python
import jax
import jax.numpy as jnp
from jax import lax
from jax.experimental import pallas as pl
from jax.experimental.pallas import tpu as pltpu
from jax.sharding import PartitionSpec as P

BF = jnp.bfloat16
F32 = jnp.float32
MESH = pl.DeviceIdType.MESH

ROWS = 24
HALF = 64
ORB = 128
COLS = 512
SLOTS = 25
REACH = 12
STEPS = 6
LONE = (
    (0, 0, 128), (0, 128, 128), (0, 256, 128), (0, 384, 128), (1, 0, 256), (1, 256, 256),
)
PIECE = 128
FIRST = len(LONE)
LAST = FIRST + STEPS - 2


def remote(src, dst, send_sem, recv_sem, device):
    return pltpu.make_async_remote_copy(
        src_ref=src, dst_ref=dst, send_sem=send_sem, recv_sem=recv_sem,
        device_id=device, device_id_type=MESH,
    )


def kernel(
    mask_h, owner_h, tn, tp, cot_h, ham_h, slope_h,
    tno, gro, fo,
    mask, owner, ext, tt, cot, ham, slope, own, xs, xr, bown, bs, br, prev, to, go, rf, fpart, fbuf, fsum,
    lsem, hsem, osem, hs, hl, hr, xss, xrs, bss, bsr, fs, fr,
):
    row = lax.axis_index("rows")
    col = lax.axis_index("cols")
    lay = lax.axis_index("layers")
    up = {"rows": lax.rem(row + 1, 16)}
    down = {"rows": lax.rem(row + 15, 16)}
    partner = {"layers": 1 - lay}
    core = lax.rem(col, 2)
    chip = lay * 2 + lax.div(col, 2)
    mate = {"cols": col + 1 - 2 * core}

    def ring(o):
        other = lax.rem(chip + o, 4)
        return {"cols": lax.rem(other, 2) * 2 + core, "layers": lax.div(other, 2)}

    def load_term():
        return pltpu.make_async_copy(tn, ext.at[pl.ds(REACH, ROWS)], lsem.at[0])

    def load_mask():
        return pltpu.make_async_copy(mask_h, mask, lsem.at[2])

    def load_owner():
        return pltpu.make_async_copy(owner_h, owner, lsem.at[3])

    load_term().start()
    barrier = pltpu.get_barrier_semaphore()
    pl.semaphore_signal(barrier, 1, device_id=up, device_id_type=MESH)
    pl.semaphore_signal(barrier, 1, device_id=down, device_id_type=MESH)
    pl.semaphore_signal(barrier, 1, device_id=mate, device_id_type=MESH)
    for o in range(1, 4):
        pl.semaphore_signal(barrier, 1, device_id=ring(o), device_id_type=MESH)

    def load_cot(part):
        at = (pl.ds(10, 4), pl.ds(0, 10), pl.ds(14, 10))[part]
        return pltpu.make_async_copy(cot_h.at[at], cot.at[at], lsem.at[4 if part else 5])

    def cot_rest():
        return pltpu.make_async_copy(
            cot_h.at[pl.ds(0, 20)], cot.at[pl.ds(0, 20)], lsem.at[4]
        )

    def load_prev():
        return pltpu.make_async_copy(tp, prev, lsem.at[1])

    def load_blocks(k):
        copies = []
        for first in (10 - 2 * k, 12 + 2 * k):
            at = pl.ds(first, 2)
            copies.append(pltpu.make_async_copy(ham_h.at[at], ham.at[at], hsem.at[k]))
            copies.append(pltpu.make_async_copy(slope_h.at[at], slope.at[at], hsem.at[k]))
        return copies

    def have_blocks(k):
        at = pl.ds(0, 8)
        pltpu.make_async_copy(ham_h.at[at], ham.at[at], hsem.at[k]).wait()

    load_mask().start()
    for c in load_blocks(0):
        c.start()
    load_cot(0).start()

    near = 1 - lax.div(lax.rem(row, 4), 2)

    def to_up(s):
        return remote(
            ext.at[pl.ds(44 - 2 * s, 2)], ext.at[pl.ds(20 - 2 * s, 2)],
            hs.at[0], hr.at[s - FIRST], up,
        )

    def to_down(s):
        return remote(
            ext.at[pl.ds(2 + 2 * s, 2)], ext.at[pl.ds(26 + 2 * s, 2)],
            hs.at[0], hr.at[s - FIRST], down,
        )

    def halo_bytes(rows, cs, sem):
        at = pl.ds(REACH, rows), slice(None), cs
        return remote(ext.at[at], ext.at[at], hs.at[0], sem, up)

    def have_piece(side, h):
        halo_bytes(2, pl.ds(PIECE * h, PIECE), hl.at[side, h]).wait_recv()

    def have_halo(s):
        halo_bytes(4, pl.ds(0, COLS), hr.at[s - FIRST]).wait_recv()

    def start_piece(h):
        cs = pl.ds(PIECE * h, PIECE)
        for side, source, target, device in ((0, 34, 10, up), (1, 12, 36, down)):
            remote(
                ext.at[pl.ds(source, 2), :, cs], ext.at[pl.ds(target, 2), :, cs],
                hs.at[0], hl.at[side, h], device,
            ).start()

    def start_halo(s):
        to_up(s).start()
        to_down(s).start()

    with jax.named_scope("rg_term"):
        load_term().wait()
    with jax.named_scope("rg_barrier"):
        pl.semaphore_wait(barrier, 6)
    start_piece(0)

    def turn(pair):
        tt[pair] = ext[pl.ds(2 * pair, 2)].reshape(ORB, COLS).T

    def turn_local(p, carry):
        turn(p + 6)
        return carry

    for u in range(1, 4):
        lax.fori_loop(4 * u - 4, 4 * u, turn_local, 0)
        start_piece(u)
    for c in load_blocks(1):
        c.start()

    def mask_rows(k, carry):
        have_blocks(k)
        for first in (10 - 2 * k, 12 + 2 * k):
            for r in range(2):
                i = first + r
                for d in range(SLOTS):
                    kept = jnp.full((HALF, ORB), mask[i, d].astype(F32), F32).astype(BF)
                    ham[i, d] = ham[i, d] * kept
                    slope[i, d] = slope[i, d] * kept
        return carry

    def step_rows(s, side):
        return 20 - 2 * s if side == 0 else 2 + 2 * s

    def send_partial(s, side):
        at = pl.ds(step_rows(s, side), 2)
        return remote(
            xs.at[at], xr.at[at], xss.at[0], xrs.at[s], partner
        )

    def stacked(i, before, after):
        w = jnp.concatenate(
            [ham[i].reshape(SLOTS * HALF, ORB), slope[i].reshape(SLOTS * HALF, ORB)],
            axis=1,
        )
        parts = [w]
        if before:
            parts = [jnp.zeros((HALF * before, 2 * ORB), BF)] + parts
        if after:
            parts = parts + [jnp.zeros((HALF * after, 2 * ORB), BF)]
        return jnp.concatenate(parts, axis=0)

    def product(pair, pairs, rows, c0=0, cols=COLS):
        cs = slice(c0, c0 + cols)
        lhs = jnp.concatenate([tt[pair + g, cs] for g in range(pairs)], axis=1)
        weights = [stacked(i, r, 2 * pairs - SLOTS - r) for i, r in rows]
        out = jnp.dot(lhs, jnp.concatenate(weights, axis=1), preferred_element_type=F32)
        for n, (i, _) in enumerate(rows):
            f = out[:, 2 * n * ORB : (2 * n + 1) * ORB].T
            low, high = f[:HALF], f[HALF:]
            own[i, :, cs] = jnp.where(lay == 0, low, high)
            xs[i, :, cs] = jnp.where(lay == 0, high, low).astype(BF)
            g = out[:, (2 * n + 1) * ORB : (2 * n + 2) * ORB]
            turned = cot[i, :, cs].T.astype(F32)
            part = 2.0 * jnp.sum(turned * g, axis=0, keepdims=True)
            rf[i] = rf[i] + part if c0 else part

    def forward_lone(u):
        other, c0, n = LONE[u]
        side = 1 - near if other else near
        cs = slice(c0, c0 + n)
        with jax.named_scope("rg_halo"):
            for h in range(c0 // PIECE, (c0 + n) // PIECE):
                have_piece(side, h)
        tt[5 + 13 * side, cs] = ext[pl.ds(10 + 26 * side, 2), :, cs].reshape(ORB, n).T
        pair = 5 + side
        product(pair, 13, ((2 * pair, 0), (2 * pair + 1, 1)), c0, n)
        at = pl.ds(2 * pair, 2), slice(None), pl.ds(c0, n)
        remote(xs.at[at], xr.at[at], xss.at[0], xrs.at[u], partner).start()

    def forward(s, carry):
        with jax.named_scope("rg_halo"):
            have_halo(s)
        turn(10 - s)
        turn(13 + s)
        for side in range(2):
            pair = 10 - s if side == 0 else 1 + s
            product(pair, 13, ((2 * pair, 0), (2 * pair + 1, 1)))

            @pl.when(s < LAST)
            def _():
                send_partial(s, side).start()

        return carry

    def push_group(g):
        i0, i1 = max(0, 4 * g - 24), min(ROWS - 1, 4 * g + 3)
        parts = []
        for i in range(i0, i1 + 1):
            d0 = 4 * g - i
            lo, hi = max(0, -d0), min(4, SLOTS - d0)
            p = []
            if lo:
                p.append(jnp.zeros((HALF * lo, ORB), BF))
            p.append(ham[i, d0 + lo : d0 + hi].reshape((hi - lo) * HALF, ORB))
            if hi < 4:
                p.append(jnp.zeros((HALF * (4 - hi), ORB), BF))
            parts.append(jnp.concatenate(p, axis=0) if len(p) > 1 else p[0])
        out = jnp.dot(
            jnp.concatenate(parts, axis=1),
            cot[i0 : i1 + 1].reshape((i1 - i0 + 1) * ORB, COLS),
            preferred_element_type=F32,
        )
        return out.reshape(4, HALF, COLS)

    def send_pushed(side, g):
        at = pl.ds(4 * g, 4)
        return remote(
            bs.at[side, at], br.at[1 - side, at], bss.at[0], bsr.at[g],
            down if side == 0 else up,
        )

    with jax.named_scope("rg_mask0"):
        load_mask().wait()
        mask_rows(0, 0)
    load_cot(1).start()
    load_cot(2).start()
    start_halo(FIRST)
    for k in range(2, STEPS):
        for c in load_blocks(k):
            c.start()
    load_prev().start()
    load_owner().start()
    load_cot(0).wait()
    with jax.named_scope("rg_fwd0"):
        for u in range(4):
            forward_lone(u)
    start_halo(FIRST + 1)
    with jax.named_scope("rg_fwd1"):
        for u in range(4, 6):
            forward_lone(u)
    start_halo(FIRST + 2)
    with jax.named_scope("rg_mask1"):
        cot_rest().wait()
        mask_rows(1, 0)
    start_halo(FIRST + 3)
    with jax.named_scope("rg_fwd2"):
        forward(FIRST, 0)
    start_halo(FIRST + 4)
    with jax.named_scope("rg_fwd3"):
        mask_rows(2, 0)
        forward(FIRST + 1, 0)
    with jax.named_scope("rg_mask2"):
        lax.fori_loop(3, STEPS, mask_rows, 0)
    with jax.named_scope("rg_edges"):
        for g in range(3):
            bs[0, 4 * g : 4 * g + 4] = push_group(g).astype(BF)
            bs[1, 4 * g : 4 * g + 4] = push_group(9 + g).astype(BF)
            send_pushed(0, g).start()
            send_pushed(1, g).start()
    with jax.named_scope("rg_fwd"):
        lax.fori_loop(FIRST + 2, LAST + 1, forward, 0)
    load_owner().wait()

    atoms = lax.broadcasted_iota(jnp.int32, (HALF, ORB), 0)
    lanes = lax.broadcasted_iota(jnp.int32, (HALF, ORB), 1)

    def gather_atoms(i, totals):
        both = []
        for total, j in zip(totals, (i, i + 12)):
            mine = jnp.where(owner[pl.ds(j, 1)] == atoms, rf[j], 0.0)
            summed = jnp.sum(mine, axis=1, keepdims=True)
            both.append(total + jnp.where(lanes == i, summed, 0.0))
        return tuple(both)

    zero = jnp.zeros((HALF, ORB), F32)
    totals = lax.fori_loop(0, 12, gather_atoms, (zero, zero))
    fpart[0] = jnp.concatenate(totals, axis=0).T[:16]

    def to_mate():
        return remote(fpart.at[0], fpart.at[1], fs.at[0], fr.at[0], mate)

    def send_force(o):
        return remote(fbuf.at[chip], fbuf.at[chip], fs.at[1], fr.at[1], ring(o))

    def all_forces():
        at = pl.ds(0, 3)
        return remote(fbuf.at[at], fbuf.at[at], fs.at[1], fr.at[1], partner)

    to_mate().start()
    with jax.named_scope("rg_push"):
        bown[0:4] = push_group(3)
    to_mate().wait()
    fbuf[chip] = fpart[0] + fpart[1]
    for o in range(1, 4):
        send_force(o).start()
    for side in range(2):
        send_partial(LAST, side).start()

    with jax.named_scope("rg_push"):
        for g in range(4, 9):
            bown[4 * (g - 3) : 4 * (g - 2)] = push_group(g)

    load_prev().wait()

    def out_term(s, side):
        at = pl.ds(step_rows(s, side), 2)
        return pltpu.make_async_copy(to.at[at], tno.at[at], osem.at[0])

    def out_middle():
        at = pl.ds(10, 4)
        return pltpu.make_async_copy(to.at[at], tno.at[at], osem.at[0])

    def out_grad(side, g):
        at = pl.ds(12 * side + 4 * g, 4)
        return pltpu.make_async_copy(go.at[at], gro.at[at], osem.at[1])

    def finish_at(at):
        both = own[at] + xr[at].astype(F32)
        to[at] = (2.0 * both - prev[at].astype(F32)).astype(BF)

    def have_partial(s, rows, cs):
        at = pl.ds(0, rows), slice(None), cs
        with jax.named_scope("rg_xW"):
            remote(xs.at[at], xr.at[at], xss.at[0], xrs.at[s], partner).wait_recv()

    def finish_term(s, carry):
        have_partial(s, 4, pl.ds(0, COLS))
        for side in range(2):
            finish_at(pl.ds(step_rows(s, side), 2))
            out_term(s, side).start()
        return carry

    def have_pushed(g):
        at = pl.ds(4 * g, 4)
        remote(bs.at[:, at], br.at[:, at], bss.at[0], bsr.at[g], up).wait_recv()

    def finish_grad(g):
        with jax.named_scope("rg_bW"):
            have_pushed(g)
        for side in range(2):
            at = pl.ds(12 * side + 4 * g, 4)
            both = bown[at] + br[side, pl.ds(4 * g, 4)].astype(F32)
            go[at] = (2.0 * both).astype(BF)
            out_grad(side, g).start()

    for u in range(FIRST):
        have_partial(u, 2, pl.ds(LONE[u][1], LONE[u][2]))
    finish_at(pl.ds(10, 4))
    out_middle().start()
    finish_grad(0)
    lax.fori_loop(FIRST, LAST - 1, finish_term, 0)
    finish_grad(1)
    finish_term(LAST - 1, 0)
    finish_grad(2)
    with jax.named_scope("rg_forceW"):
        all_forces().wait_recv()
    summed = fbuf[0]
    for s in range(1, 4):
        summed = summed + fbuf[s]
    fsum[0:12] = summed[:12, :HALF]
    fsum[12:24] = summed[:12, HALF:]
    force_out = pltpu.make_async_copy(fsum, fo, osem.at[2])
    force_out.start()

    with jax.named_scope("rg_sent"):
        sent = ext.at[pl.ds(0, ROWS)]
        remote(sent, sent, hs.at[0], hr.at[0], up).wait_send()
        remote(bs, br, bss.at[0], bsr.at[0], up).wait_send()
        all_forces().wait_send()
        force_out.wait()
        pltpu.make_async_copy(go, gro, osem.at[1]).wait()
    with jax.named_scope("rg_last"):
        finish_term(LAST, 0)
    with jax.named_scope("rg_tail"):
        remote(xs, xr, xss.at[0], xrs.at[0], partner).wait_send()
        pltpu.make_async_copy(to, tno, osem.at[0]).wait()


def write_out(a, b, c, ao, bo, co, sem):
    copies = [pltpu.make_async_copy(c, co, sem.at[0])]
    for x, y in ((a, ao), (b, bo)):
        for part in range(8):
            at = pl.ds(3 * part, 3)
            copies.append(pltpu.make_async_copy(x.at[at], y.at[at], sem.at[0]))
    for copy in copies:
        copy.start()
    for copy in copies:
        copy.wait()


def local(term_now, term_prev, cotangent, ham_blocks, block_mask, ham_slope, atom_owner):
    anyspace = pl.BlockSpec(memory_space=pl.ANY)
    dma = pltpu.SemaphoreType.DMA
    block = (ROWS, HALF, COLS)
    shapes = ((block, BF), (block, BF), ((ROWS, HALF), F32))
    results = pl.pallas_call(
        kernel,
        out_shape=tuple(pltpu.VMEM(*s) for s in shapes),
        in_specs=[anyspace] * 7,
        out_specs=(anyspace,) * 3,
        scratch_shapes=[
            pltpu.SMEM((ROWS, SLOTS), jnp.int32),
            pltpu.VMEM((ROWS, ORB), jnp.int32),
            pltpu.VMEM((ROWS + 2 * REACH, HALF, COLS), BF),
            pltpu.VMEM((24, COLS, ORB), BF),
            pltpu.VMEM((ROWS, ORB, COLS), BF),
            pltpu.VMEM((ROWS, SLOTS, HALF, ORB), BF),
            pltpu.VMEM((ROWS, SLOTS, HALF, ORB), BF),
            pltpu.VMEM(block, F32),
            pltpu.VMEM(block, BF),
            pltpu.VMEM(block, BF),
            pltpu.VMEM(block, F32),
            pltpu.VMEM((2, REACH, HALF, COLS), BF),
            pltpu.VMEM((2, REACH, HALF, COLS), BF),
            pltpu.VMEM(block, BF),
            pltpu.VMEM(block, BF),
            pltpu.VMEM(block, BF),
            pltpu.VMEM((ROWS, 1, ORB), F32),
            pltpu.VMEM((2, 16, ORB), F32),
            pltpu.VMEM((4, 16, ORB), F32),
            pltpu.VMEM((ROWS, HALF), F32),
            dma((6,)), dma((STEPS,)), dma((3,)),
            dma((1,)), dma((2, COLS // PIECE)), dma((STEPS - 1,)),
            dma((1,)), dma((LAST + 1,)),
            dma((1,)), dma((3,)),
            dma((2,)), dma((2,)),
        ],
        compiler_params=pltpu.CompilerParams(
            collective_id=0, has_side_effects=True, vmem_limit_bytes=54_000_000
        ),
        name="chebyshev",
    )(block_mask, atom_owner, term_now, term_prev, cotangent, ham_blocks, ham_slope)
    return pl.pallas_call(
        write_out,
        out_shape=tuple(jax.ShapeDtypeStruct(*s) for s in shapes),
        in_specs=[anyspace] * 3,
        out_specs=(anyspace,) * 3,
        scratch_shapes=[dma((1,))],
        compiler_params=pltpu.CompilerParams(vmem_limit_bytes=4_000_000),
        name="write_out",
    )(*results)


def solution(mesh):
    return jax.shard_map(
        local,
        mesh=mesh,
        in_specs=(
            P("rows", "layers", "cols"),
            P("rows", "layers", "cols"),
            P("rows", None, "cols"),
            P("rows", None, "layers", None),
            P("rows", None),
            P("rows", None, "layers", None),
            P("rows", None),
        ),
        out_specs=(P("rows", "layers", "cols"), P("rows", "layers", "cols"), P("rows", None)),
        check_vma=False,
    )
```

```python
import jax
import jax.numpy as jnp
from jax import lax
from jax.experimental import pallas as pl
from jax.experimental.pallas import tpu as pltpu
from jax.sharding import PartitionSpec as P

BF = jnp.bfloat16
F32 = jnp.float32
MESH = pl.DeviceIdType.MESH

ROWS = 24
HALF = 64
ORB = 128
COLS = 512
SLOTS = 25
REACH = 12
STEPS = 6
LONE = (
    (0, 0, 128), (0, 128, 128), (0, 256, 128), (0, 384, 128),
    (1, 0, 128), (1, 128, 128), (1, 256, 128), (1, 384, 128),
)
PIECE = 128
FIRST = len(LONE)
LAST = FIRST + STEPS - 2


def remote(src, dst, send_sem, recv_sem, device):
    return pltpu.make_async_remote_copy(
        src_ref=src, dst_ref=dst, send_sem=send_sem, recv_sem=recv_sem,
        device_id=device, device_id_type=MESH,
    )


def kernel(
    mask_h, owner_h, tn, tp, cot_h, ham_h, slope_h,
    tno, gro, fo,
    mask, owner, ext, tt, cot, ham, slope, own, xs, xr, bown, bs, br, prev, to, go, rf, fpart, fbuf, fsum,
    lsem, hsem, osem, hs, hl, hr, xss, xrs, bss, bsr, fs, fr,
):
    row = lax.axis_index("rows")
    col = lax.axis_index("cols")
    lay = lax.axis_index("layers")
    up = {"rows": lax.rem(row + 1, 16)}
    down = {"rows": lax.rem(row + 15, 16)}
    partner = {"layers": 1 - lay}
    core = lax.rem(col, 2)
    chip = lay * 2 + lax.div(col, 2)
    mate = {"cols": col + 1 - 2 * core}

    def ring(o):
        other = lax.rem(chip + o, 4)
        return {"cols": lax.rem(other, 2) * 2 + core, "layers": lax.div(other, 2)}

    def load_term():
        return pltpu.make_async_copy(tn, ext.at[pl.ds(REACH, ROWS)], lsem.at[0])

    def load_mask():
        return pltpu.make_async_copy(mask_h, mask, lsem.at[2])

    def load_owner():
        return pltpu.make_async_copy(owner_h, owner, lsem.at[3])

    load_term().start()
    barrier = pltpu.get_barrier_semaphore()
    pl.semaphore_signal(barrier, 1, device_id=up, device_id_type=MESH)
    pl.semaphore_signal(barrier, 1, device_id=down, device_id_type=MESH)
    pl.semaphore_signal(barrier, 1, device_id=mate, device_id_type=MESH)
    for o in range(1, 4):
        pl.semaphore_signal(barrier, 1, device_id=ring(o), device_id_type=MESH)

    def load_cot(part):
        at = (pl.ds(10, 4), pl.ds(0, 10), pl.ds(14, 10))[part]
        return pltpu.make_async_copy(cot_h.at[at], cot.at[at], lsem.at[4 if part else 5])

    def cot_rest():
        return pltpu.make_async_copy(
            cot_h.at[pl.ds(0, 20)], cot.at[pl.ds(0, 20)], lsem.at[4]
        )

    def load_prev():
        return pltpu.make_async_copy(tp, prev, lsem.at[1])

    def load_blocks(k):
        copies = []
        for first in (10 - 2 * k, 12 + 2 * k):
            at = pl.ds(first, 2)
            copies.append(pltpu.make_async_copy(ham_h.at[at], ham.at[at], hsem.at[k]))
            copies.append(pltpu.make_async_copy(slope_h.at[at], slope.at[at], hsem.at[k]))
        return copies

    def have_blocks(k):
        at = pl.ds(0, 8)
        pltpu.make_async_copy(ham_h.at[at], ham.at[at], hsem.at[k]).wait()

    load_mask().start()
    for c in load_blocks(0):
        c.start()
    load_cot(0).start()

    near = 1 - lax.div(lax.rem(row, 4), 2)

    def to_up(s):
        return remote(
            ext.at[pl.ds(48 - 2 * s, 2)], ext.at[pl.ds(24 - 2 * s, 2)],
            hs.at[0], hr.at[s - FIRST], up,
        )

    def to_down(s):
        return remote(
            ext.at[pl.ds(2 * s - 2, 2)], ext.at[pl.ds(22 + 2 * s, 2)],
            hs.at[0], hr.at[s - FIRST], down,
        )

    def halo_bytes(rows, cs, sem):
        at = pl.ds(REACH, rows), slice(None), cs
        return remote(ext.at[at], ext.at[at], hs.at[0], sem, up)

    def have_piece(side, h):
        halo_bytes(2, pl.ds(PIECE * h, PIECE), hl.at[side, h]).wait_recv()

    def have_halo(s):
        halo_bytes(4, pl.ds(0, COLS), hr.at[s - FIRST]).wait_recv()

    def start_piece(h):
        cs = pl.ds(PIECE * h, PIECE)
        for side, source, target, device in ((0, 34, 10, up), (1, 12, 36, down)):
            remote(
                ext.at[pl.ds(source, 2), :, cs], ext.at[pl.ds(target, 2), :, cs],
                hs.at[0], hl.at[side, h], device,
            ).start()

    def start_halo(s):
        to_up(s).start()
        to_down(s).start()

    with jax.named_scope("rg_term"):
        load_term().wait()
    with jax.named_scope("rg_barrier"):
        pl.semaphore_wait(barrier, 6)
    start_piece(0)

    def turn(pair):
        tt[pair] = ext[pl.ds(2 * pair, 2)].reshape(ORB, COLS).T

    def turn_local(p, carry):
        turn(p + 6)
        return carry

    for u in range(1, 4):
        lax.fori_loop(4 * u - 4, 4 * u, turn_local, 0)
        start_piece(u)
    for c in load_blocks(1):
        c.start()

    def mask_rows(k, carry):
        have_blocks(k)
        for first in (10 - 2 * k, 12 + 2 * k):
            for r in range(2):
                i = first + r
                for d in range(SLOTS):
                    kept = jnp.full((HALF, ORB), mask[i, d].astype(F32), F32).astype(BF)
                    ham[i, d] = ham[i, d] * kept
                    slope[i, d] = slope[i, d] * kept
        return carry

    def step_rows(s, side):
        return 24 - 2 * s if side == 0 else 2 * s - 2

    def send_partial(s, side):
        at = pl.ds(step_rows(s, side), 2)
        return remote(
            xs.at[at], xr.at[at], xss.at[0], xrs.at[s], partner
        )

    def stacked(i, before, after):
        w = jnp.concatenate(
            [ham[i].reshape(SLOTS * HALF, ORB), slope[i].reshape(SLOTS * HALF, ORB)],
            axis=1,
        )
        parts = [w]
        if before:
            parts = [jnp.zeros((HALF * before, 2 * ORB), BF)] + parts
        if after:
            parts = parts + [jnp.zeros((HALF * after, 2 * ORB), BF)]
        return jnp.concatenate(parts, axis=0)

    def product(pair, pairs, rows, c0=0, cols=COLS):
        cs = slice(c0, c0 + cols)
        lhs = jnp.concatenate([tt[pair + g, cs] for g in range(pairs)], axis=1)
        weights = [stacked(i, r, 2 * pairs - SLOTS - r) for i, r in rows]
        out = jnp.dot(lhs, jnp.concatenate(weights, axis=1), preferred_element_type=F32)
        for n, (i, _) in enumerate(rows):
            f = out[:, 2 * n * ORB : (2 * n + 1) * ORB].T
            low, high = f[:HALF], f[HALF:]
            own[i, :, cs] = jnp.where(lay == 0, low, high)
            xs[i, :, cs] = jnp.where(lay == 0, high, low).astype(BF)
            g = out[:, (2 * n + 1) * ORB : (2 * n + 2) * ORB]
            turned = cot[i, :, cs].T.astype(F32)
            part = 2.0 * jnp.sum(turned * g, axis=0, keepdims=True)
            rf[i] = rf[i] + part if c0 else part

    def forward_lone(u):
        other, c0, n = LONE[u]
        side = 1 - near if other else near
        cs = slice(c0, c0 + n)
        with jax.named_scope("rg_halo"):
            for h in range(c0 // PIECE, (c0 + n) // PIECE):
                have_piece(side, h)
        tt[5 + 13 * side, cs] = ext[pl.ds(10 + 26 * side, 2), :, cs].reshape(ORB, n).T
        pair = 5 + side
        product(pair, 13, ((2 * pair, 0), (2 * pair + 1, 1)), c0, n)
        at = pl.ds(2 * pair, 2), slice(None), pl.ds(c0, n)
        remote(xs.at[at], xr.at[at], xss.at[0], xrs.at[u], partner).start()

    def forward(s, carry):
        with jax.named_scope("rg_halo"):
            have_halo(s)
        turn(12 - s)
        turn(11 + s)
        for side in range(2):
            pair = 12 - s if side == 0 else s - 1
            product(pair, 13, ((2 * pair, 0), (2 * pair + 1, 1)))

            @pl.when(s < LAST)
            def _():
                send_partial(s, side).start()

        return carry

    def push_group(g):
        i0, i1 = max(0, 4 * g - 24), min(ROWS - 1, 4 * g + 3)
        parts = []
        for i in range(i0, i1 + 1):
            d0 = 4 * g - i
            lo, hi = max(0, -d0), min(4, SLOTS - d0)
            p = []
            if lo:
                p.append(jnp.zeros((HALF * lo, ORB), BF))
            p.append(ham[i, d0 + lo : d0 + hi].reshape((hi - lo) * HALF, ORB))
            if hi < 4:
                p.append(jnp.zeros((HALF * (4 - hi), ORB), BF))
            parts.append(jnp.concatenate(p, axis=0) if len(p) > 1 else p[0])
        out = jnp.dot(
            jnp.concatenate(parts, axis=1),
            cot[i0 : i1 + 1].reshape((i1 - i0 + 1) * ORB, COLS),
            preferred_element_type=F32,
        )
        return out.reshape(4, HALF, COLS)

    def send_pushed(side, g):
        at = pl.ds(4 * g, 4)
        return remote(
            bs.at[side, at], br.at[1 - side, at], bss.at[0], bsr.at[g],
            down if side == 0 else up,
        )

    with jax.named_scope("rg_mask0"):
        load_mask().wait()
        mask_rows(0, 0)
    load_cot(1).start()
    load_cot(2).start()
    start_halo(FIRST)
    for k in range(2, STEPS):
        for c in load_blocks(k):
            c.start()
    load_prev().start()
    load_owner().start()
    load_cot(0).wait()
    with jax.named_scope("rg_fwd0"):
        for u in range(4):
            forward_lone(u)
    start_halo(FIRST + 1)
    with jax.named_scope("rg_fwd1"):
        for u in range(4, 8):
            forward_lone(u)
    start_halo(FIRST + 2)
    with jax.named_scope("rg_mask1"):
        cot_rest().wait()
        mask_rows(1, 0)
    start_halo(FIRST + 3)
    with jax.named_scope("rg_fwd2"):
        forward(FIRST, 0)
    start_halo(FIRST + 4)
    with jax.named_scope("rg_fwd3"):
        mask_rows(2, 0)
        forward(FIRST + 1, 0)
    with jax.named_scope("rg_mask2"):
        lax.fori_loop(3, STEPS, mask_rows, 0)
    with jax.named_scope("rg_edges"):
        for g in range(3):
            bs[0, 4 * g : 4 * g + 4] = push_group(g).astype(BF)
            bs[1, 4 * g : 4 * g + 4] = push_group(9 + g).astype(BF)
            send_pushed(0, g).start()
            send_pushed(1, g).start()
    with jax.named_scope("rg_fwd"):
        lax.fori_loop(FIRST + 2, LAST + 1, forward, 0)
    load_owner().wait()

    atoms = lax.broadcasted_iota(jnp.int32, (HALF, ORB), 0)
    lanes = lax.broadcasted_iota(jnp.int32, (HALF, ORB), 1)

    def gather_atoms(i, totals):
        both = []
        for total, j in zip(totals, (i, i + 12)):
            mine = jnp.where(owner[pl.ds(j, 1)] == atoms, rf[j], 0.0)
            summed = jnp.sum(mine, axis=1, keepdims=True)
            both.append(total + jnp.where(lanes == i, summed, 0.0))
        return tuple(both)

    zero = jnp.zeros((HALF, ORB), F32)
    totals = lax.fori_loop(0, 12, gather_atoms, (zero, zero))
    fpart[0] = jnp.concatenate(totals, axis=0).T[:16]

    def to_mate():
        return remote(fpart.at[0], fpart.at[1], fs.at[0], fr.at[0], mate)

    def send_force(o):
        return remote(fbuf.at[chip], fbuf.at[chip], fs.at[1], fr.at[1], ring(o))

    def all_forces():
        at = pl.ds(0, 3)
        return remote(fbuf.at[at], fbuf.at[at], fs.at[1], fr.at[1], partner)

    to_mate().start()
    with jax.named_scope("rg_push"):
        bown[0:4] = push_group(3)
    to_mate().wait()
    fbuf[chip] = fpart[0] + fpart[1]
    for o in range(1, 4):
        send_force(o).start()
    for side in range(2):
        send_partial(LAST, side).start()

    with jax.named_scope("rg_push"):
        for g in range(4, 9):
            bown[4 * (g - 3) : 4 * (g - 2)] = push_group(g)

    load_prev().wait()

    def out_term(s, side):
        at = pl.ds(step_rows(s, side), 2)
        return pltpu.make_async_copy(to.at[at], tno.at[at], osem.at[0])

    def out_middle():
        at = pl.ds(10, 4)
        return pltpu.make_async_copy(to.at[at], tno.at[at], osem.at[0])

    def out_grad(side, g):
        at = pl.ds(12 * side + 4 * g, 4)
        return pltpu.make_async_copy(go.at[at], gro.at[at], osem.at[1])

    def finish_at(at):
        both = own[at] + xr[at].astype(F32)
        to[at] = (2.0 * both - prev[at].astype(F32)).astype(BF)

    def have_partial(s, rows, cs):
        at = pl.ds(0, rows), slice(None), cs
        with jax.named_scope("rg_xW"):
            remote(xs.at[at], xr.at[at], xss.at[0], xrs.at[s], partner).wait_recv()

    def finish_term(s, carry):
        have_partial(s, 4, pl.ds(0, COLS))
        for side in range(2):
            finish_at(pl.ds(step_rows(s, side), 2))
            out_term(s, side).start()
        return carry

    def have_pushed(g):
        at = pl.ds(4 * g, 4)
        remote(bs.at[:, at], br.at[:, at], bss.at[0], bsr.at[g], up).wait_recv()

    def finish_grad(g):
        with jax.named_scope("rg_bW"):
            have_pushed(g)
        for side in range(2):
            at = pl.ds(12 * side + 4 * g, 4)
            both = bown[at] + br[side, pl.ds(4 * g, 4)].astype(F32)
            go[at] = (2.0 * both).astype(BF)
            out_grad(side, g).start()

    for u in range(FIRST):
        have_partial(u, 2, pl.ds(LONE[u][1], LONE[u][2]))
    finish_at(pl.ds(10, 4))
    out_middle().start()
    finish_grad(0)
    lax.fori_loop(FIRST, LAST - 1, finish_term, 0)
    finish_grad(1)
    finish_term(LAST - 1, 0)
    finish_grad(2)
    with jax.named_scope("rg_forceW"):
        all_forces().wait_recv()
    summed = fbuf[0]
    for s in range(1, 4):
        summed = summed + fbuf[s]
    fsum[0:12] = summed[:12, :HALF]
    fsum[12:24] = summed[:12, HALF:]
    force_out = pltpu.make_async_copy(fsum, fo, osem.at[2])
    force_out.start()

    with jax.named_scope("rg_sent"):
        sent = ext.at[pl.ds(0, ROWS)]
        remote(sent, sent, hs.at[0], hr.at[0], up).wait_send()
        remote(bs, br, bss.at[0], bsr.at[0], up).wait_send()
        all_forces().wait_send()
        force_out.wait()
        pltpu.make_async_copy(go, gro, osem.at[1]).wait()
    with jax.named_scope("rg_last"):
        finish_term(LAST, 0)
    with jax.named_scope("rg_tail"):
        remote(xs, xr, xss.at[0], xrs.at[0], partner).wait_send()
        pltpu.make_async_copy(to, tno, osem.at[0]).wait()


def write_out(a, b, c, ao, bo, co, sem):
    copies = [pltpu.make_async_copy(c, co, sem.at[0])]
    for x, y in ((a, ao), (b, bo)):
        for part in range(8):
            at = pl.ds(3 * part, 3)
            copies.append(pltpu.make_async_copy(x.at[at], y.at[at], sem.at[0]))
    for copy in copies:
        copy.start()
    for copy in copies:
        copy.wait()


def local(term_now, term_prev, cotangent, ham_blocks, block_mask, ham_slope, atom_owner):
    anyspace = pl.BlockSpec(memory_space=pl.ANY)
    dma = pltpu.SemaphoreType.DMA
    block = (ROWS, HALF, COLS)
    shapes = ((block, BF), (block, BF), ((ROWS, HALF), F32))
    results = pl.pallas_call(
        kernel,
        out_shape=tuple(pltpu.VMEM(*s) for s in shapes),
        in_specs=[anyspace] * 7,
        out_specs=(anyspace,) * 3,
        scratch_shapes=[
            pltpu.SMEM((ROWS, SLOTS), jnp.int32),
            pltpu.VMEM((ROWS, ORB), jnp.int32),
            pltpu.VMEM((ROWS + 2 * REACH, HALF, COLS), BF),
            pltpu.VMEM((24, COLS, ORB), BF),
            pltpu.VMEM((ROWS, ORB, COLS), BF),
            pltpu.VMEM((ROWS, SLOTS, HALF, ORB), BF),
            pltpu.VMEM((ROWS, SLOTS, HALF, ORB), BF),
            pltpu.VMEM(block, F32),
            pltpu.VMEM(block, BF),
            pltpu.VMEM(block, BF),
            pltpu.VMEM(block, F32),
            pltpu.VMEM((2, REACH, HALF, COLS), BF),
            pltpu.VMEM((2, REACH, HALF, COLS), BF),
            pltpu.VMEM(block, BF),
            pltpu.VMEM(block, BF),
            pltpu.VMEM(block, BF),
            pltpu.VMEM((ROWS, 1, ORB), F32),
            pltpu.VMEM((2, 16, ORB), F32),
            pltpu.VMEM((4, 16, ORB), F32),
            pltpu.VMEM((ROWS, HALF), F32),
            dma((6,)), dma((STEPS,)), dma((3,)),
            dma((1,)), dma((2, COLS // PIECE)), dma((STEPS - 1,)),
            dma((1,)), dma((LAST + 1,)),
            dma((1,)), dma((3,)),
            dma((2,)), dma((2,)),
        ],
        compiler_params=pltpu.CompilerParams(
            collective_id=0, has_side_effects=True, vmem_limit_bytes=54_000_000
        ),
        name="chebyshev",
    )(block_mask, atom_owner, term_now, term_prev, cotangent, ham_blocks, ham_slope)
    return pl.pallas_call(
        write_out,
        out_shape=tuple(jax.ShapeDtypeStruct(*s) for s in shapes),
        in_specs=[anyspace] * 3,
        out_specs=(anyspace,) * 3,
        scratch_shapes=[dma((1,))],
        compiler_params=pltpu.CompilerParams(vmem_limit_bytes=4_000_000),
        name="write_out",
    )(*results)


def solution(mesh):
    return jax.shard_map(
        local,
        mesh=mesh,
        in_specs=(
            P("rows", "layers", "cols"),
            P("rows", "layers", "cols"),
            P("rows", None, "cols"),
            P("rows", None, "layers", None),
            P("rows", None),
            P("rows", None, "layers", None),
            P("rows", None),
        ),
        out_specs=(P("rows", "layers", "cols"), P("rows", "layers", "cols"), P("rows", None)),
        check_vma=False,
    )
```

```python
import jax
import jax.numpy as jnp
from jax import lax
from jax.experimental import pallas as pl
from jax.experimental.pallas import tpu as pltpu
from jax.sharding import PartitionSpec as P

BF = jnp.bfloat16
F32 = jnp.float32
MESH = pl.DeviceIdType.MESH

ROWS = 24
HALF = 64
ORB = 128
COLS = 512
SLOTS = 25
REACH = 12
STEPS = 6
LONE = (
    (0, 0, 128), (0, 128, 128), (0, 256, 128), (0, 384, 128),
    (1, 0, 128), (1, 128, 128), (1, 256, 128), (1, 384, 128),
)
PIECE = 128
FIRST = len(LONE)
LAST = FIRST + STEPS - 2


def remote(src, dst, send_sem, recv_sem, device):
    return pltpu.make_async_remote_copy(
        src_ref=src, dst_ref=dst, send_sem=send_sem, recv_sem=recv_sem,
        device_id=device, device_id_type=MESH,
    )


def kernel(
    mask_h, owner_h, tn, tp, cot_h, ham_h, slope_h,
    tno, gro, fo,
    mask, owner, ext, tt, cot, ham, slope, own, xs, xr, bown, bs, br, prev, to, go, rf, fpart, fbuf, fsum,
    lsem, hsem, osem, hs, hl, hr, xss, xrs, bss, bsr, fs, fr,
):
    row = lax.axis_index("rows")
    col = lax.axis_index("cols")
    lay = lax.axis_index("layers")
    up = {"rows": lax.rem(row + 1, 16)}
    down = {"rows": lax.rem(row + 15, 16)}
    partner = {"layers": 1 - lay}
    core = lax.rem(col, 2)
    chip = lay * 2 + lax.div(col, 2)
    mate = {"cols": col + 1 - 2 * core}

    def ring(o):
        other = lax.rem(chip + o, 4)
        return {"cols": lax.rem(other, 2) * 2 + core, "layers": lax.div(other, 2)}

    def load_term():
        return pltpu.make_async_copy(tn, ext.at[pl.ds(REACH, ROWS)], lsem.at[0])

    def load_mask():
        return pltpu.make_async_copy(mask_h, mask, lsem.at[2])

    def load_owner():
        return pltpu.make_async_copy(owner_h, owner, lsem.at[3])

    load_term().start()
    barrier = pltpu.get_barrier_semaphore()
    pl.semaphore_signal(barrier, 1, device_id=up, device_id_type=MESH)
    pl.semaphore_signal(barrier, 1, device_id=down, device_id_type=MESH)
    pl.semaphore_signal(barrier, 1, device_id=mate, device_id_type=MESH)
    for o in range(1, 4):
        pl.semaphore_signal(barrier, 1, device_id=ring(o), device_id_type=MESH)

    def load_cot(part):
        at = (pl.ds(10, 4), pl.ds(0, 10), pl.ds(14, 10))[part]
        return pltpu.make_async_copy(cot_h.at[at], cot.at[at], lsem.at[4 if part else 5])

    def cot_rest():
        return pltpu.make_async_copy(
            cot_h.at[pl.ds(0, 20)], cot.at[pl.ds(0, 20)], lsem.at[4]
        )

    def load_prev():
        return pltpu.make_async_copy(tp, prev, lsem.at[1])

    def load_blocks(k):
        copies = []
        for first in (10 - 2 * k, 12 + 2 * k):
            at = pl.ds(first, 2)
            copies.append(pltpu.make_async_copy(ham_h.at[at], ham.at[at], hsem.at[k]))
            copies.append(pltpu.make_async_copy(slope_h.at[at], slope.at[at], hsem.at[k]))
        return copies

    def have_blocks(k):
        at = pl.ds(0, 8)
        pltpu.make_async_copy(ham_h.at[at], ham.at[at], hsem.at[k]).wait()

    load_mask().start()
    for c in load_blocks(0):
        c.start()
    load_cot(0).start()

    near = 1 - lax.div(lax.rem(row, 4), 2)

    def to_up(s):
        return remote(
            ext.at[pl.ds(48 - 2 * s, 2)], ext.at[pl.ds(24 - 2 * s, 2)],
            hs.at[0], hr.at[0, s - FIRST], up,
        )

    def to_down(s):
        return remote(
            ext.at[pl.ds(2 * s - 2, 2)], ext.at[pl.ds(22 + 2 * s, 2)],
            hs.at[0], hr.at[1, s - FIRST], down,
        )

    def halo_bytes(rows, cs, sem):
        at = pl.ds(REACH, rows), slice(None), cs
        return remote(ext.at[at], ext.at[at], hs.at[0], sem, up)

    def have_piece(side, h):
        halo_bytes(2, pl.ds(PIECE * h, PIECE), hl.at[side, h]).wait_recv()

    def have_halo(side, s):
        halo_bytes(2, pl.ds(0, COLS), hr.at[side, s - FIRST]).wait_recv()

    def start_piece(h):
        cs = pl.ds(PIECE * h, PIECE)
        for side, source, target, device in ((0, 34, 10, up), (1, 12, 36, down)):
            remote(
                ext.at[pl.ds(source, 2), :, cs], ext.at[pl.ds(target, 2), :, cs],
                hs.at[0], hl.at[side, h], device,
            ).start()

    def start_halo(s):
        to_up(s).start()
        to_down(s).start()

    with jax.named_scope("rg_term"):
        load_term().wait()
    with jax.named_scope("rg_barrier"):
        pl.semaphore_wait(barrier, 6)
    start_piece(0)

    def turn(pair):
        tt[pair] = ext[pl.ds(2 * pair, 2)].reshape(ORB, COLS).T

    def turn_local(p, carry):
        turn(p + 6)
        return carry

    for u in range(1, 4):
        lax.fori_loop(4 * u - 4, 4 * u, turn_local, 0)
        start_piece(u)
    for c in load_blocks(1):
        c.start()

    def mask_rows(k, carry):
        have_blocks(k)
        for first in (10 - 2 * k, 12 + 2 * k):
            for r in range(2):
                i = first + r
                for d in range(SLOTS):
                    kept = jnp.full((HALF, ORB), mask[i, d].astype(F32), F32).astype(BF)
                    ham[i, d] = ham[i, d] * kept
                    slope[i, d] = slope[i, d] * kept
        return carry

    def step_rows(s, side):
        return 24 - 2 * s if side == 0 else 2 * s - 2

    def send_partial(s, side):
        at = pl.ds(step_rows(s, side), 2)
        return remote(
            xs.at[at], xr.at[at], xss.at[0], xrs.at[s], partner
        )

    def stacked(i, before, after):
        w = jnp.concatenate(
            [ham[i].reshape(SLOTS * HALF, ORB), slope[i].reshape(SLOTS * HALF, ORB)],
            axis=1,
        )
        parts = [w]
        if before:
            parts = [jnp.zeros((HALF * before, 2 * ORB), BF)] + parts
        if after:
            parts = parts + [jnp.zeros((HALF * after, 2 * ORB), BF)]
        return jnp.concatenate(parts, axis=0)

    def product(pair, pairs, rows, c0=0, cols=COLS):
        cs = slice(c0, c0 + cols)
        lhs = jnp.concatenate([tt[pair + g, cs] for g in range(pairs)], axis=1)
        weights = [stacked(i, r, 2 * pairs - SLOTS - r) for i, r in rows]
        out = jnp.dot(lhs, jnp.concatenate(weights, axis=1), preferred_element_type=F32)
        for n, (i, _) in enumerate(rows):
            f = out[:, 2 * n * ORB : (2 * n + 1) * ORB].T
            low, high = f[:HALF], f[HALF:]
            own[i, :, cs] = jnp.where(lay == 0, low, high)
            xs[i, :, cs] = jnp.where(lay == 0, high, low).astype(BF)
            g = out[:, (2 * n + 1) * ORB : (2 * n + 2) * ORB]
            turned = cot[i, :, cs].T.astype(F32)
            part = 2.0 * jnp.sum(turned * g, axis=0, keepdims=True)
            rf[i] = rf[i] + part if c0 else part

    def forward_lone(u):
        other, c0, n = LONE[u]
        side = 1 - near if other else near
        cs = slice(c0, c0 + n)
        with jax.named_scope("rg_halo"):
            for h in range(c0 // PIECE, (c0 + n) // PIECE):
                have_piece(side, h)
        tt[5 + 13 * side, cs] = ext[pl.ds(10 + 26 * side, 2), :, cs].reshape(ORB, n).T
        pair = 5 + side
        product(pair, 13, ((2 * pair, 0), (2 * pair + 1, 1)), c0, n)
        at = pl.ds(2 * pair, 2), slice(None), pl.ds(c0, n)
        remote(xs.at[at], xr.at[at], xss.at[0], xrs.at[u], partner).start()

    def forward(s, carry):
        for side in (near, 1 - near):
            with jax.named_scope("rg_halo"):
                have_halo(side, s)
            turn((12 - s) * (1 - side) + (11 + s) * side)
            pair = (12 - s) * (1 - side) + (s - 1) * side
            product(pair, 13, ((2 * pair, 0), (2 * pair + 1, 1)))

            @pl.when(s < LAST)
            def _():
                at = pl.ds(2 * pair, 2)
                remote(xs.at[at], xr.at[at], xss.at[0], xrs.at[s], partner).start()

        return carry

    def push_group(g):
        i0, i1 = max(0, 4 * g - 24), min(ROWS - 1, 4 * g + 3)
        parts = []
        for i in range(i0, i1 + 1):
            d0 = 4 * g - i
            lo, hi = max(0, -d0), min(4, SLOTS - d0)
            p = []
            if lo:
                p.append(jnp.zeros((HALF * lo, ORB), BF))
            p.append(ham[i, d0 + lo : d0 + hi].reshape((hi - lo) * HALF, ORB))
            if hi < 4:
                p.append(jnp.zeros((HALF * (4 - hi), ORB), BF))
            parts.append(jnp.concatenate(p, axis=0) if len(p) > 1 else p[0])
        out = jnp.dot(
            jnp.concatenate(parts, axis=1),
            cot[i0 : i1 + 1].reshape((i1 - i0 + 1) * ORB, COLS),
            preferred_element_type=F32,
        )
        return out.reshape(4, HALF, COLS)

    def send_pushed(side, g):
        at = pl.ds(4 * g, 4)
        return remote(
            bs.at[side, at], br.at[1 - side, at], bss.at[0], bsr.at[g],
            down if side == 0 else up,
        )

    with jax.named_scope("rg_mask0"):
        load_mask().wait()
        mask_rows(0, 0)
    load_cot(1).start()
    load_cot(2).start()
    start_halo(FIRST)
    for k in range(2, STEPS):
        for c in load_blocks(k):
            c.start()
    load_prev().start()
    load_owner().start()
    load_cot(0).wait()
    with jax.named_scope("rg_fwd0"):
        for u in range(4):
            forward_lone(u)
    start_halo(FIRST + 1)
    with jax.named_scope("rg_fwd1"):
        for u in range(4, 8):
            forward_lone(u)
    start_halo(FIRST + 2)
    with jax.named_scope("rg_mask1"):
        cot_rest().wait()
        mask_rows(1, 0)
    start_halo(FIRST + 3)
    with jax.named_scope("rg_fwd2"):
        forward(FIRST, 0)
    start_halo(FIRST + 4)
    with jax.named_scope("rg_fwd3"):
        mask_rows(2, 0)
        forward(FIRST + 1, 0)
    with jax.named_scope("rg_mask2"):
        lax.fori_loop(3, STEPS, mask_rows, 0)
    with jax.named_scope("rg_edges"):
        for g in range(3):
            bs[0, 4 * g : 4 * g + 4] = push_group(g).astype(BF)
            bs[1, 4 * g : 4 * g + 4] = push_group(9 + g).astype(BF)
            send_pushed(0, g).start()
            send_pushed(1, g).start()
    with jax.named_scope("rg_fwd"):
        lax.fori_loop(FIRST + 2, LAST + 1, forward, 0)
    load_owner().wait()

    atoms = lax.broadcasted_iota(jnp.int32, (HALF, ORB), 0)
    lanes = lax.broadcasted_iota(jnp.int32, (HALF, ORB), 1)

    def gather_atoms(i, totals):
        both = []
        for total, j in zip(totals, (i, i + 12)):
            mine = jnp.where(owner[pl.ds(j, 1)] == atoms, rf[j], 0.0)
            summed = jnp.sum(mine, axis=1, keepdims=True)
            both.append(total + jnp.where(lanes == i, summed, 0.0))
        return tuple(both)

    zero = jnp.zeros((HALF, ORB), F32)
    totals = lax.fori_loop(0, 12, gather_atoms, (zero, zero))
    fpart[0] = jnp.concatenate(totals, axis=0).T[:16]

    def to_mate():
        return remote(fpart.at[0], fpart.at[1], fs.at[0], fr.at[0], mate)

    def send_force(o):
        return remote(fbuf.at[chip], fbuf.at[chip], fs.at[1], fr.at[1], ring(o))

    def all_forces():
        at = pl.ds(0, 3)
        return remote(fbuf.at[at], fbuf.at[at], fs.at[1], fr.at[1], partner)

    to_mate().start()
    with jax.named_scope("rg_push"):
        bown[0:4] = push_group(3)
    to_mate().wait()
    fbuf[chip] = fpart[0] + fpart[1]
    for o in range(1, 4):
        send_force(o).start()
    for side in range(2):
        send_partial(LAST, side).start()

    with jax.named_scope("rg_push"):
        for g in range(4, 9):
            bown[4 * (g - 3) : 4 * (g - 2)] = push_group(g)

    load_prev().wait()

    def out_term(s, side):
        at = pl.ds(step_rows(s, side), 2)
        return pltpu.make_async_copy(to.at[at], tno.at[at], osem.at[0])

    def out_middle():
        at = pl.ds(10, 4)
        return pltpu.make_async_copy(to.at[at], tno.at[at], osem.at[0])

    def out_grad(side, g):
        at = pl.ds(12 * side + 4 * g, 4)
        return pltpu.make_async_copy(go.at[at], gro.at[at], osem.at[1])

    def finish_at(at):
        both = own[at] + xr[at].astype(F32)
        to[at] = (2.0 * both - prev[at].astype(F32)).astype(BF)

    def have_partial(s, rows, cs):
        at = pl.ds(0, rows), slice(None), cs
        with jax.named_scope("rg_xW"):
            remote(xs.at[at], xr.at[at], xss.at[0], xrs.at[s], partner).wait_recv()

    def finish_term(s, carry):
        have_partial(s, 4, pl.ds(0, COLS))
        for side in range(2):
            finish_at(pl.ds(step_rows(s, side), 2))
            out_term(s, side).start()
        return carry

    def have_pushed(g):
        at = pl.ds(4 * g, 4)
        remote(bs.at[:, at], br.at[:, at], bss.at[0], bsr.at[g], up).wait_recv()

    def finish_grad(g):
        with jax.named_scope("rg_bW"):
            have_pushed(g)
        for side in range(2):
            at = pl.ds(12 * side + 4 * g, 4)
            both = bown[at] + br[side, pl.ds(4 * g, 4)].astype(F32)
            go[at] = (2.0 * both).astype(BF)
            out_grad(side, g).start()

    for u in range(FIRST):
        have_partial(u, 2, pl.ds(LONE[u][1], LONE[u][2]))
    finish_at(pl.ds(10, 4))
    out_middle().start()
    finish_grad(0)
    lax.fori_loop(FIRST, LAST - 1, finish_term, 0)
    finish_grad(1)
    finish_term(LAST - 1, 0)
    finish_grad(2)
    with jax.named_scope("rg_forceW"):
        all_forces().wait_recv()
    summed = fbuf[0]
    for s in range(1, 4):
        summed = summed + fbuf[s]
    fsum[0:12] = summed[:12, :HALF]
    fsum[12:24] = summed[:12, HALF:]
    force_out = pltpu.make_async_copy(fsum, fo, osem.at[2])
    force_out.start()

    with jax.named_scope("rg_sent"):
        sent = ext.at[pl.ds(0, ROWS)]
        remote(sent, sent, hs.at[0], hr.at[0, 0], up).wait_send()
        remote(bs, br, bss.at[0], bsr.at[0], up).wait_send()
        all_forces().wait_send()
        force_out.wait()
        pltpu.make_async_copy(go, gro, osem.at[1]).wait()
    with jax.named_scope("rg_last"):
        finish_term(LAST, 0)
    with jax.named_scope("rg_tail"):
        remote(xs, xr, xss.at[0], xrs.at[0], partner).wait_send()
        pltpu.make_async_copy(to, tno, osem.at[0]).wait()


def write_out(a, b, c, ao, bo, co, sem):
    copies = [pltpu.make_async_copy(c, co, sem.at[0])]
    for x, y in ((a, ao), (b, bo)):
        for part in range(8):
            at = pl.ds(3 * part, 3)
            copies.append(pltpu.make_async_copy(x.at[at], y.at[at], sem.at[0]))
    for copy in copies:
        copy.start()
    for copy in copies:
        copy.wait()


def local(term_now, term_prev, cotangent, ham_blocks, block_mask, ham_slope, atom_owner):
    anyspace = pl.BlockSpec(memory_space=pl.ANY)
    dma = pltpu.SemaphoreType.DMA
    block = (ROWS, HALF, COLS)
    shapes = ((block, BF), (block, BF), ((ROWS, HALF), F32))
    results = pl.pallas_call(
        kernel,
        out_shape=tuple(pltpu.VMEM(*s) for s in shapes),
        in_specs=[anyspace] * 7,
        out_specs=(anyspace,) * 3,
        scratch_shapes=[
            pltpu.SMEM((ROWS, SLOTS), jnp.int32),
            pltpu.VMEM((ROWS, ORB), jnp.int32),
            pltpu.VMEM((ROWS + 2 * REACH, HALF, COLS), BF),
            pltpu.VMEM((24, COLS, ORB), BF),
            pltpu.VMEM((ROWS, ORB, COLS), BF),
            pltpu.VMEM((ROWS, SLOTS, HALF, ORB), BF),
            pltpu.VMEM((ROWS, SLOTS, HALF, ORB), BF),
            pltpu.VMEM(block, F32),
            pltpu.VMEM(block, BF),
            pltpu.VMEM(block, BF),
            pltpu.VMEM(block, F32),
            pltpu.VMEM((2, REACH, HALF, COLS), BF),
            pltpu.VMEM((2, REACH, HALF, COLS), BF),
            pltpu.VMEM(block, BF),
            pltpu.VMEM(block, BF),
            pltpu.VMEM(block, BF),
            pltpu.VMEM((ROWS, 1, ORB), F32),
            pltpu.VMEM((2, 16, ORB), F32),
            pltpu.VMEM((4, 16, ORB), F32),
            pltpu.VMEM((ROWS, HALF), F32),
            dma((6,)), dma((STEPS,)), dma((3,)),
            dma((1,)), dma((2, COLS // PIECE)), dma((2, STEPS - 1)),
            dma((1,)), dma((LAST + 1,)),
            dma((1,)), dma((3,)),
            dma((2,)), dma((2,)),
        ],
        compiler_params=pltpu.CompilerParams(
            collective_id=0, has_side_effects=True, vmem_limit_bytes=54_000_000
        ),
        name="chebyshev",
    )(block_mask, atom_owner, term_now, term_prev, cotangent, ham_blocks, ham_slope)
    return pl.pallas_call(
        write_out,
        out_shape=tuple(jax.ShapeDtypeStruct(*s) for s in shapes),
        in_specs=[anyspace] * 3,
        out_specs=(anyspace,) * 3,
        scratch_shapes=[dma((1,))],
        compiler_params=pltpu.CompilerParams(vmem_limit_bytes=4_000_000),
        name="write_out",
    )(*results)


def solution(mesh):
    return jax.shard_map(
        local,
        mesh=mesh,
        in_specs=(
            P("rows", "layers", "cols"),
            P("rows", "layers", "cols"),
            P("rows", None, "cols"),
            P("rows", None, "layers", None),
            P("rows", None),
            P("rows", None, "layers", None),
            P("rows", None),
        ),
        out_specs=(P("rows", "layers", "cols"), P("rows", "layers", "cols"), P("rows", None)),
        check_vma=False,
    )
```
